32 devices in a mesh: pairs: 2 (over y), blk: 8 (over z, x), panel: 2 (over core).
Axes of the slice: x: 2, y: 2, z: 4, core: 2. Of those that a mesh axis runs over, the one named last changes fastest.
Arguments:
- first_frame: bfloat16 [4096, 256], P(('pairs', 'blk', 'panel')), parts along dimension 0, may hold values from -8 to 8
- second_frame: bfloat16 [16, 8, 16, 256], P(('pairs', 'blk'), None, 'panel'), parts along dimension 0, may hold values from -8 to 8
Outputs:
- matched: float32 [4, 2, 4096], P(None, None, ('pairs', 'blk', 'panel')), parts along dimension 2
- energy: float32 [4, 4096], P(None, ('pairs', 'blk', 'panel')), parts along dimension 1
The draws below stay inside these ranges and needn't reach their ends.
There are 2 independent parts, one for each index of `pairs`. The reference program is written for one: setup_inputs(seed, part) draws one part's arguments, and reference() takes and returns one part's arrays. A program takes and returns all parts, laid end to end along the dimension named above; each array names one. Nothing has to cross between parts.
All inputs are finite; a program needn't handle non-finite values.
Results may differ from the reference program's by a relative error of at most 0.014.
Values may be sent and summed in bfloat16 or wider, within the bound.
A program may use at most 128 MiB of HBM per device.

```python
import math
import jax
import jax.numpy as jnp
from jax import lax

C = 256
LEVELS = 4
COLBLK = 8
BCOLS = 16
BAND = 8
KEYBLK = 8
H2 = 8
W2 = 128
Q = 2048


def draw_first_frame(key, part):
    noise_key = jax.random.fold_in(jax.random.fold_in(key, 11), 0)
    values = jax.random.truncated_normal(noise_key, -4.0, 4.0, (Q, C), jnp.float32)
    return values.astype(jnp.bfloat16)


def draw_second_frame(key, part):
    noise_key = jax.random.fold_in(jax.random.fold_in(key, 23), 0)
    shape = (KEYBLK, BAND, BCOLS, C)
    values = jax.random.truncated_normal(noise_key, -4.0, 4.0, shape, jnp.float32)
    return values.astype(jnp.bfloat16)


def setup_inputs(seed: int = 0, part: int = 0) -> dict:
    seeds = jax.random.split(jax.random.key(seed), 3)
    part_splits = jax.random.split(jax.random.fold_in(seeds[2], part), 3)
    first_frame = draw_first_frame(jax.random.fold_in(jax.random.fold_in(seeds[2], part), 71), part)
    second_frame = draw_second_frame(jax.random.fold_in(jax.random.fold_in(seeds[2], part), 71), part)
    return {"first_frame": first_frame, "second_frame": second_frame}


def grid_of(second_frame):
    row_blocks = KEYBLK // COLBLK
    blocked = second_frame.reshape(row_blocks, COLBLK, BAND, BCOLS, C)
    return jnp.transpose(blocked, (0, 2, 1, 3, 4)).reshape(H2, W2, C)

def build_levels(grid):
    result = [grid]
    pooled = grid.astype(jnp.float32)
    for level_index in range(1, LEVELS):
        rows_now, cols_now, channels = pooled.shape
        pooled = pooled.reshape(rows_now // 2, 2, cols_now // 2, 2, channels).mean(axis=(1, 3))
        result.append(pooled.astype(jnp.bfloat16))
    return result

def position_table(row_count, col_count, level_index):
    row_grid = jnp.broadcast_to(jnp.arange(row_count, dtype=jnp.float32)[:, None], (row_count, col_count))
    col_grid = jnp.broadcast_to(jnp.arange(col_count, dtype=jnp.float32)[None, :], (row_count, col_count))
    spacing = 2.0 ** level_index
    row_pos = (row_grid + 0.5) * (spacing / H2)
    col_pos = (col_grid + 0.5) * (spacing / W2)
    unit_row = jnp.ones_like(row_pos)
    return jnp.stack([unit_row.reshape(-1), row_pos.reshape(-1), col_pos.reshape(-1)])

def reference(first_frame, second_frame):
    levels = build_levels(grid_of(second_frame))
    block_rows = math.gcd(Q, 1024)
    query_blocks = first_frame.reshape(Q // block_rows, block_rows, C)
    energies = []
    matches = []
    for level_index in range(LEVELS):
        level_grid = levels[level_index]
        row_count = level_grid.shape[0]
        col_count = level_grid.shape[1]
        key_rows = level_grid.reshape(row_count * col_count, C)
        table = position_table(row_count, col_count, level_index)
        factor = 3.0 * 2.0 ** level_index / math.sqrt(C)

        def per_block(queries, key_rows=key_rows, table=table, factor=factor):
            scores = jnp.dot(queries, key_rows.T, preferred_element_type=jnp.float32) * factor
            maxima = lax.optimization_barrier(jnp.max(scores, axis=1))
            weights = jnp.exp(scores - maxima[:, None])
            totals = jnp.dot(table, weights.T, precision=lax.Precision.HIGHEST, preferred_element_type=jnp.float32)
            return (maxima, totals)
        maxima, totals = lax.map(per_block, query_blocks)
        maxima = maxima.reshape(Q)
        totals = jnp.transpose(totals, (1, 0, 2)).reshape(3, Q)
        energies.append(maxima + jnp.log(totals[0]))
        matches.append(totals[1:] / totals[0:1])
    return (jnp.stack(matches), jnp.stack(energies))
```

```python
import functools
import math

import jax
import jax.numpy as jnp
from jax import lax
from jax.experimental import pallas as pl
from jax.experimental.pallas import tpu as pltpu
from jax.sharding import PartitionSpec as P

LEVELS = 4
COLBLK = 8
BCOLS = 16
INNER = 2
NEG = -1e30
MESH = pl.DeviceIdType.MESH


def absorb(raw, sources, rows, cols, total_rows, total_cols, rates, state, lane):
    n = len(sources)
    q = raw.shape[-1]
    col = lax.broadcasted_iota(jnp.int32, (cols, q), 0)
    values = raw.reshape(n, rows, cols, q)
    for level in range(LEVELS):
        step = 2**level
        if level:
            pairs = values.reshape(n, rows // step, 2, cols, q)
            values = pairs[:, :, 0] + pairs[:, :, 1]
            values = values + pltpu.roll(values, step // 2, 2)
        height = rows // step
        old = state[level, 0, :, lane]
        top = jnp.maximum(old, jnp.max(values, axis=(0, 1)))
        weights = jnp.exp2((values - top) * rates[level])
        decay = jnp.exp2((old - top) * rates[level])
        col_in = ((col >> level).astype(jnp.float32) + 0.5) * (step / total_cols)
        total = state[level, 1, :, lane] * decay
        row_sum = state[level, 2, :, lane] * decay
        col_sum = state[level, 3, :, lane] * decay
        for s, (row_base, col_base) in enumerate(sources):
            part = weights[s, 0]
            part_row = weights[s, 0] * (0.5 * step / total_rows)
            for i in range(1, height):
                part = part + weights[s, i]
                part_row = part_row + weights[s, i] * ((i + 0.5) * step / total_rows)
            total = total + part
            row_sum = row_sum + (part_row + part * row_base)
            col_sum = col_sum + part * (col_in + col_base)
        state[level, 0, :, lane] = top
        state[level, 1, :, lane] = total
        state[level, 2, :, lane] = row_sum
        state[level, 3, :, lane] = col_sum


def settle(cols, rates, state, lane):
    tops, totals, row_sums, col_sums = [], [], [], []
    for level in range(LEVELS):
        step = 2**level
        top = state[level, 0, :, lane]
        col = lax.broadcasted_iota(jnp.int32, top.shape, 0)
        valid = (col & (step - 1)) == step - 1
        best = jnp.max(jnp.where(valid, top, NEG), axis=0, keepdims=True)
        scale = jnp.exp2((top - best) * rates[level])
        for rows_out, i in ((totals, 1), (row_sums, 2), (col_sums, 3)):
            term = jnp.where(valid, state[level, i, :, lane] * scale, 0.0)
            rows_out.append(jnp.sum(term, axis=0, keepdims=True))
        tops.append(best * (rates[level] * math.log(2.0)))
    return jnp.concatenate(tops + totals + row_sums + col_sums, axis=0)


def merge(one, two):
    top = jnp.maximum(one[:LEVELS], two[:LEVELS])
    one_scale, two_scale = jnp.exp(one[:LEVELS] - top), jnp.exp(two[:LEVELS] - top)
    sums = [one[LEVELS * i : LEVELS * (i + 1)] * one_scale + two[LEVELS * i : LEVELS * (i + 1)] * two_scale
            for i in (1, 2, 3)]
    return jnp.concatenate([top] + sums, axis=0)


def kernel(dims, q_ref, k_ref, merged_ref, qbuf, kbuf, state, done, got, ready,
           k_send, k_recv, l_send, q_send, q_recv, r_send, r_recv):
    blk, panels, rows, cols = dims
    outer = blk // INNER
    queries = q_ref.shape[0]
    total_rows, total_cols = rows * blk // COLBLK, BCOLS * COLBLK
    chip, core = lax.axis_index("blk"), lax.axis_index("panel")
    me = chip * panels + core
    hub = panels - 1
    line, spot = chip // INNER, chip % INNER
    mate = line * INNER + (INNER - 1 - spot)
    barrier = pltpu.get_barrier_semaphore()

    def at(where, side):
        return {"blk": where, "panel": side}

    def each(low, high, step):
        lax.fori_loop(low, high, lambda i, _: (step(i), 0)[1], 0)

    def key_copy(where):
        return pltpu.make_async_remote_copy(
            k_ref, kbuf.at[me], k_send.at[where], k_recv.at[me],
            device_id=at(where, hub), device_id_type=MESH)

    def below(act):
        @pl.when(spot != 0)
        def _():
            act(key_copy(0))
        each(0, line, lambda i: act(key_copy(i * INNER + spot)))

    def tile(i):
        return pl.ds(i * queries, queries)

    def query_copy(where, place, sem):
        return pltpu.make_async_remote_copy(
            q_ref, qbuf.at[tile(place)], q_send.at[sem], q_recv.at[place],
            device_id=at(where, hub), device_id_type=MESH)

    def lift(where):
        return [pltpu.make_async_remote_copy(
            kbuf.at[chip * panels + side], kbuf.at[chip * panels + side],
            l_send.at[where * panels + side], k_recv.at[chip * panels + side],
            device_id=at(where, hub), device_id_type=MESH) for side in range(panels)]

    def lend():
        return [pltpu.make_async_remote_copy(
            qbuf.at[tile(side)], qbuf.at[tile(panels + side)], q_send.at[side], q_recv.at[panels + side],
            device_id=at(mate, hub), device_id_type=MESH) for side in range(panels)]

    def result_copy(where, place, side):
        return pltpu.make_async_remote_copy(
            done.at[place * panels + side], got.at[place], r_send.at[place * panels + side], r_recv.at[place],
            device_id=at(where, side), device_id_type=MESH)

    def key_landed(slot):
        pltpu.make_async_copy(k_ref, kbuf.at[slot], k_recv.at[slot]).wait()

    def query_landed(place):
        pltpu.make_async_copy(q_ref, qbuf.at[tile(place)], q_recv.at[place]).wait()

    def result_landed(place):
        pltpu.make_async_copy(done.at[place], got.at[place], r_recv.at[place]).wait()

    lends = (spot == 0) & (chip != 0)
    holds = chip != 1

    @pl.when(core == hub)
    def _():
        own_k = pltpu.make_async_copy(k_ref, kbuf.at[me], k_recv.at[me])
        own_q = pltpu.make_async_copy(q_ref, qbuf.at[tile(hub)], q_recv.at[hub])
        for side in range(hub):
            pl.semaphore_signal(barrier, inc=1, device_id=at(chip, side), device_id_type=MESH)

        def greet(where):
            for side in range(panels):
                pl.semaphore_signal(barrier, inc=1, device_id=at(where, side), device_id_type=MESH)

        def answer(where):
            pl.semaphore_signal(ready.at[chip], inc=1, device_id=at(where, hub), device_id_type=MESH)

        each(line + 1, outer, lambda i: greet(i * INNER + spot))

        @pl.when(chip == 0)
        def _():
            each(0, outer, lambda i: greet(i * INNER + 1))

        @pl.when(lends)
        def _():
            greet(mate)

        @pl.when(chip != 0)
        def _():
            pl.semaphore_wait(barrier, line + jnp.where(spot != 0, jnp.where(line > 0, 2, 1), 0))

        below(lambda copy: copy.start())

        @pl.when(spot != 0)
        def _():
            query_copy(mate, panels + hub, 1).start()

            @pl.when(chip != 1)
            def _():
                answer(mate)

        each(0, line, lambda i: answer(i * INNER + spot))
        own_k.start()
        own_q.start()
        state[:, 0] = jnp.full_like(state[:, 0], NEG)
        state[:, 1:] = jnp.zeros_like(state[:, 1:])
        for side in range(panels):
            key_landed(chip * panels + side)
            query_landed(side)

        @pl.when(lends)
        def _():
            pl.semaphore_wait(ready.at[mate], 1)
            for copy in lend():
                copy.start()

        def send_up(i):
            where = i * INNER + spot
            pl.semaphore_wait(ready.at[where], 1)
            for copy in lift(where):
                copy.start()

        each(line + 1, outer, send_up)

        @pl.when(holds)
        def _():
            for side in range(panels):
                query_landed(panels + side)

        rates = [3.0 / math.sqrt(k_ref.shape[-1]) / math.log(2.0) / 2**level for level in range(LEVELS)]

        def take(turn):
            upper = line >= (outer + 1) // 2
            place = jnp.where(upper, outer - 1 - line, line)
            pick = jnp.where(turn == 0, place, jnp.where(turn <= place, turn - 1, turn))
            pick = jnp.where(upper, outer - 1 - pick, pick)
            source = jnp.where(chip == 0, turn, pick * INNER + spot)

            @pl.when(source != chip)
            def _():
                for side in range(panels):
                    key_landed(source * panels + side)

            row_base = (source // COLBLK).astype(jnp.float32) * (rows / total_rows)
            left = (source % COLBLK) * BCOLS
            sources = [(row_base, (left + side * cols).astype(jnp.float32) * (1.0 / total_cols))
                       for side in range(panels)]

            def score(half):
                keys = kbuf[pl.ds(source * panels, panels)].reshape(panels * rows * cols, kbuf.shape[-1])
                raw = lax.dot_general(keys, qbuf[pl.ds(half * panels * queries, panels * queries)],
                                      (((1,), (1,)), ((), ())), preferred_element_type=jnp.float32)
                for side in range(panels):
                    lane = pl.ds((half * panels + side) * queries, queries)
                    absorb(raw[:, side * queries : (side + 1) * queries], sources, rows, cols,
                           total_rows, total_cols, rates, state, lane)

            @pl.when(holds & (source % INNER == spot))
            def _():
                score(1)

            score(0)

        each(0, jnp.where(chip == 0, blk, outer), take)

        @pl.when(holds)
        def _():
            for side in range(panels):
                done[panels + side] = settle(cols, rates, state, tile(panels + side))
                result_copy(mate, 1, side).start()

        for side in range(hub):
            done[side] = settle(cols, rates, state, tile(side))
            result_copy(chip, 0, side).start()
        done[hub] = settle(cols, rates, state, tile(hub))

        @pl.when(chip == 0)
        def _():
            merged_ref[...] = done[hub]

        @pl.when(chip != 0)
        def _():
            result_landed(1)
            merged_ref[...] = merge(done[hub], got[1])

        for side in range(hub):
            result_copy(chip, 0, side).wait_send()

        @pl.when(holds)
        def _():
            for side in range(panels):
                result_copy(mate, 1, side).wait_send()

        @pl.when(lends)
        def _():
            for copy in lend():
                copy.wait_send()

        @pl.when(spot != 0)
        def _():
            query_copy(mate, panels + hub, 1).wait_send()

        below(lambda copy: copy.wait_send())
        each(line + 1, outer, lambda i: [copy.wait_send() for copy in lift(i * INNER + spot)])

    @pl.when(core != hub)
    def _():
        pl.semaphore_wait(barrier, line + jnp.where(spot != 0, jnp.where(line > 0, 3, 2), 1))
        below(lambda copy: copy.start())

        @pl.when(spot != 0)
        def _():
            query_copy(mate, panels + core, 1).start()

        key_copy(chip).start()
        query_copy(chip, core, 0).start()

        @pl.when(chip != 0)
        def _():
            result_landed(1)

        result_landed(0)

        @pl.when(chip == 0)
        def _():
            merged_ref[...] = got[0]

        @pl.when(chip != 0)
        def _():
            merged_ref[...] = merge(got[0], got[1])

        @pl.when(spot != 0)
        def _():
            query_copy(mate, panels + core, 1).wait_send()

        key_copy(chip).wait_send()
        query_copy(chip, core, 0).wait_send()
        below(lambda copy: copy.wait_send())


def finish(merged_ref, matched_ref, energy_ref):
    top, total = merged_ref[:LEVELS], merged_ref[LEVELS : 2 * LEVELS]
    energy_ref[...] = top + jnp.log(total)
    matched_ref[:, 0, :] = merged_ref[2 * LEVELS : 3 * LEVELS] / total
    matched_ref[:, 1, :] = merged_ref[3 * LEVELS :] / total


def body(blk, panels, first_frame, second_frame):
    queries, channels = first_frame.shape
    _, rows, cols, _ = second_frame.shape
    keys = second_frame.reshape(rows * cols, channels)
    dma = pltpu.SemaphoreType.DMA
    merged = pl.pallas_call(
        functools.partial(kernel, (blk, panels, rows, cols)),
        out_shape=pltpu.VMEM((4 * LEVELS, queries), jnp.float32),
        in_specs=[pl.BlockSpec(memory_space=pl.ANY)] * 2,
        out_specs=pl.BlockSpec(memory_space=pltpu.VMEM),
        scratch_shapes=[
            pltpu.VMEM((2 * panels * queries, channels), jnp.bfloat16),
            pltpu.VMEM((blk * panels, rows * cols, channels), jnp.bfloat16),
            pltpu.VMEM((LEVELS, 4, cols, 2 * panels * queries), jnp.float32),
            pltpu.VMEM((2 * panels, 4 * LEVELS, queries), jnp.float32),
            pltpu.VMEM((2, 4 * LEVELS, queries), jnp.float32),
            pltpu.SemaphoreType.REGULAR((blk,)),
            dma((blk,)), dma((blk * panels,)), dma((blk * panels,)),
            dma((panels,)), dma((2 * panels,)),
            dma((2 * panels,)), dma((2,)),
        ],
        compiler_params=pltpu.CompilerParams(collective_id=0, has_side_effects=True),
        name="corr",
    )(first_frame, keys)
    return pl.pallas_call(
        finish,
        out_shape=(jax.ShapeDtypeStruct((LEVELS, 2, queries), jnp.float32),
                   jax.ShapeDtypeStruct((LEVELS, queries), jnp.float32)),
        in_specs=[pl.BlockSpec(memory_space=pltpu.VMEM)],
        out_specs=(pl.BlockSpec(memory_space=pltpu.VMEM), pl.BlockSpec(memory_space=pltpu.VMEM)),
        name="finish",
    )(pltpu.with_memory_space_constraint(merged, pltpu.VMEM))


def solution(mesh):
    placed = (P(("pairs", "blk", "panel"), None), P(("pairs", "blk"), None, "panel", None))
    return jax.shard_map(
        functools.partial(body, mesh.shape["blk"], mesh.shape["panel"]),
        mesh=mesh,
        in_specs=placed,
        out_specs=(P(None, None, ("pairs", "blk", "panel")), P(None, ("pairs", "blk", "panel"))),
        check_vma=False,
    )
```

```python
import functools
import math

import jax
import jax.numpy as jnp
from jax import lax
from jax.experimental import pallas as pl
from jax.experimental.pallas import tpu as pltpu
from jax.sharding import PartitionSpec as P

LEVELS = 4
COLBLK = 8
BCOLS = 16
INNER = 2
NEG = -1e30
MESH = pl.DeviceIdType.MESH


def absorb(raw, sources, rows, cols, total_rows, total_cols, rates, state, lane):
    n = len(sources)
    q = raw.shape[-1]
    col = lax.broadcasted_iota(jnp.int32, (cols, q), 0)
    values = raw.reshape(n, rows, cols, q)
    for level in range(LEVELS):
        step = 2**level
        if level:
            pairs = values.reshape(n, rows // step, 2, cols, q)
            values = pairs[:, :, 0] + pairs[:, :, 1]
            values = values + pltpu.roll(values, step // 2, 2)
        height = rows // step
        old = state[level, 0, :, lane]
        top = jnp.maximum(old, jnp.max(values, axis=(0, 1)))
        weights = jnp.exp2((values - top) * rates[level])
        decay = jnp.exp2((old - top) * rates[level])
        col_in = ((col >> level).astype(jnp.float32) + 0.5) * (step / total_cols)
        total = state[level, 1, :, lane] * decay
        row_sum = state[level, 2, :, lane] * decay
        col_sum = state[level, 3, :, lane] * decay
        for s, (row_base, col_base) in enumerate(sources):
            part = weights[s, 0]
            part_row = weights[s, 0] * (0.5 * step / total_rows)
            for i in range(1, height):
                part = part + weights[s, i]
                part_row = part_row + weights[s, i] * ((i + 0.5) * step / total_rows)
            total = total + part
            row_sum = row_sum + (part_row + part * row_base)
            col_sum = col_sum + part * (col_in + col_base)
        state[level, 0, :, lane] = top
        state[level, 1, :, lane] = total
        state[level, 2, :, lane] = row_sum
        state[level, 3, :, lane] = col_sum


def settle(cols, rates, state, lane):
    tops, totals, row_sums, col_sums = [], [], [], []
    for level in range(LEVELS):
        step = 2**level
        top = state[level, 0, :, lane]
        col = lax.broadcasted_iota(jnp.int32, top.shape, 0)
        valid = (col & (step - 1)) == step - 1
        best = jnp.max(jnp.where(valid, top, NEG), axis=0, keepdims=True)
        scale = jnp.exp2((top - best) * rates[level])
        for rows_out, i in ((totals, 1), (row_sums, 2), (col_sums, 3)):
            term = jnp.where(valid, state[level, i, :, lane] * scale, 0.0)
            rows_out.append(jnp.sum(term, axis=0, keepdims=True))
        tops.append(best * (rates[level] * math.log(2.0)))
    return jnp.concatenate(tops + totals + row_sums + col_sums, axis=0)


def merge(one, two):
    top = jnp.maximum(one[:LEVELS], two[:LEVELS])
    one_scale, two_scale = jnp.exp(one[:LEVELS] - top), jnp.exp(two[:LEVELS] - top)
    sums = [one[LEVELS * i : LEVELS * (i + 1)] * one_scale + two[LEVELS * i : LEVELS * (i + 1)] * two_scale
            for i in (1, 2, 3)]
    return jnp.concatenate([top] + sums, axis=0)


def kernel(dims, q_ref, k_ref, merged_ref, qbuf, kbuf, state, done, got, ready,
           k_send, k_recv, l_send, q_send, q_recv, r_send, r_recv):
    blk, panels, rows, cols = dims
    outer = blk // INNER
    queries = q_ref.shape[0]
    keys = rows * cols
    total_rows, total_cols = rows * blk // COLBLK, BCOLS * COLBLK
    chip, core = lax.axis_index("blk"), lax.axis_index("panel")
    me = chip * panels + core
    hub = panels - 1
    line, spot = chip // INNER, chip % INNER
    mate = line * INNER + (INNER - 1 - spot)
    last = blk - 1
    barrier = pltpu.get_barrier_semaphore()
    rates = [3.0 / math.sqrt(k_ref.shape[-1]) / math.log(2.0) / 2**level for level in range(LEVELS)]

    def at(where, side):
        return {"blk": where, "panel": side}

    def each(low, high, step):
        lax.fori_loop(low, high, lambda i, _: (step(i), 0)[1], 0)

    def tile(i):
        return pl.ds(i * queries, queries)

    def key_copy(where, side=hub):
        return pltpu.make_async_remote_copy(
            k_ref, kbuf.at[me], k_send.at[where if side == hub else blk], k_recv.at[me],
            device_id=at(where, side), device_id_type=MESH)

    def below(act):
        @pl.when(chip == last)
        def _():
            @pl.when(core != hub)
            def _():
                act(key_copy(0, 0))

            act(key_copy(0))

        def step(i):
            swap = (chip == last) & (i < 2)
            act(key_copy(jnp.where(swap, 1 - i, i) * INNER + spot))

        each(0, line, step)

    def query_copy(where, place, sem):
        return pltpu.make_async_remote_copy(
            q_ref, qbuf.at[tile(place)], q_send.at[sem], q_recv.at[place],
            device_id=at(where, hub), device_id_type=MESH)

    def lift(where):
        return [pltpu.make_async_remote_copy(
            kbuf.at[chip * panels + side], kbuf.at[chip * panels + side],
            l_send.at[where * panels + side], k_recv.at[chip * panels + side],
            device_id=at(where, hub), device_id_type=MESH) for side in range(panels)]

    def lend():
        return [pltpu.make_async_remote_copy(
            qbuf.at[tile(side)], qbuf.at[tile(panels + side)], q_send.at[side], q_recv.at[panels + side],
            device_id=at(mate, hub), device_id_type=MESH) for side in range(panels)]

    def result_copy(where, place, side):
        return pltpu.make_async_remote_copy(
            done.at[place * panels + side], got.at[place], r_send.at[place * panels + side], r_recv.at[place],
            device_id=at(where, side), device_id_type=MESH)

    def key_landed(slot):
        pltpu.make_async_copy(k_ref, kbuf.at[slot], k_recv.at[slot]).wait()

    def query_landed(place):
        pltpu.make_async_copy(q_ref, qbuf.at[tile(place)], q_recv.at[place]).wait()

    def result_landed(place):
        pltpu.make_async_copy(done.at[place], got.at[place], r_recv.at[place]).wait()

    def score(source, sides, tiles):
        row_base = (source // COLBLK).astype(jnp.float32) * (rows / total_rows)
        left = (source % COLBLK) * BCOLS
        sources = [(row_base, (left + side * cols).astype(jnp.float32) * (1.0 / total_cols)) for side in sides]
        block = kbuf[pl.ds(source * panels + sides[0], len(sides))].reshape(len(sides) * keys, kbuf.shape[-1])
        raw = lax.dot_general(block, qbuf[: tiles * queries], (((1,), (1,)), ((), ())),
                              preferred_element_type=jnp.float32)
        for i in range(tiles):
            absorb(raw[:, i * queries : (i + 1) * queries], sources, rows, cols,
                   total_rows, total_cols, rates, state, tile(i))

    def clear():
        state[:, 0] = jnp.full_like(state[:, 0], NEG)
        state[:, 1:] = jnp.zeros_like(state[:, 1:])

    def partial(place):
        return settle(cols, rates, state, tile(place))

    greeted = line + jnp.where(spot != 0, 1, 0) + jnp.where(chip == last, panels, 0)

    @pl.when(core == hub)
    def _():
        own_k = pltpu.make_async_copy(k_ref, kbuf.at[me], k_recv.at[me])
        own_q = pltpu.make_async_copy(q_ref, qbuf.at[tile(hub)], q_recv.at[hub])

        def greet(where):
            for side in range(panels):
                pl.semaphore_signal(barrier, inc=1, device_id=at(where, side), device_id_type=MESH)

        def answer(where):
            pl.semaphore_signal(ready.at[chip], inc=1, device_id=at(where, hub), device_id_type=MESH)

        for side in range(hub):
            pl.semaphore_signal(barrier, inc=1, device_id=at(chip, side), device_id_type=MESH)

        @pl.when(spot == 0)
        def _():
            greet(mate)

        each(line + 1, outer, lambda i: greet(i * INNER + spot))

        @pl.when(chip == 0)
        def _():
            greet(last)

        @pl.when(chip != 0)
        def _():
            pl.semaphore_wait(barrier, greeted)

        below(lambda copy: copy.start())

        @pl.when(spot != 0)
        def _():
            query_copy(mate, panels + hub, 1).start()
            answer(mate)

        each(0, line, lambda i: answer(i * INNER + spot))
        own_k.start()
        own_q.start()
        clear()
        for side in range(panels):
            query_landed(side)

        @pl.when(spot == 0)
        def _():
            pl.semaphore_wait(ready.at[mate], 1)
            for copy in lend():
                copy.start()

        for side in range(panels):
            key_landed(chip * panels + side)

        def send_up(i):
            where = i * INNER + spot
            pl.semaphore_wait(ready.at[where], 1)
            for copy in lift(where):
                copy.start()

        each(line + 1, outer, send_up)
        for side in range(panels):
            query_landed(panels + side)

        def take(turn):
            upper = line >= (outer + 1) // 2
            place = jnp.where(upper, outer - 1 - line, line)
            pick = jnp.where(turn == 0, place, jnp.where(turn <= place, turn - 1, turn))
            pick = jnp.where(upper, outer - 1 - pick, pick)
            source = pick * INNER + spot

            @pl.when(source != chip)
            def _():
                for side in range(panels):
                    key_landed(source * panels + side)

            score(source, range(panels), 2 * panels)

        each(0, jnp.where(chip == 1, outer - 1, outer), take)
        for side in range(panels):
            done[panels + side] = partial(panels + side)
            result_copy(mate, 1, side).start()

        def late(side):
            key_landed(last * panels + side)
            score(jnp.int32(last), [side], panels)

        def return_rest():
            for side in range(hub):
                done[side] = partial(side)
                result_copy(chip, 0, side).start()

        @pl.when(line == 0)
        def _():
            late(hub)

            @pl.when(chip == 0)
            def _():
                return_rest()

            late(0)

        @pl.when(chip != 0)
        def _():
            return_rest()

        own = partial(hub)
        result_landed(1)
        merged_ref[...] = merge(own, got[1])

        for side in range(hub):
            result_copy(chip, 0, side).wait_send()
        for side in range(panels):
            result_copy(mate, 1, side).wait_send()

        @pl.when(spot == 0)
        def _():
            for copy in lend():
                copy.wait_send()

        @pl.when(spot != 0)
        def _():
            query_copy(mate, panels + hub, 1).wait_send()

        below(lambda copy: copy.wait_send())
        each(line + 1, outer, lambda i: [copy.wait_send() for copy in lift(i * INNER + spot)])

    @pl.when(core != hub)
    def _():
        @pl.when(chip == 0)
        def _():
            for side in range(panels):
                pl.semaphore_signal(barrier, inc=1, device_id=at(last, side), device_id_type=MESH)

        pl.semaphore_wait(barrier, greeted + 1)
        below(lambda copy: copy.start())

        @pl.when(spot != 0)
        def _():
            query_copy(mate, panels + core, 1).start()

        query_copy(chip, core, 0).start()
        key_copy(chip).start()

        @pl.when(chip == 0)
        def _():
            own_q = pltpu.make_async_copy(q_ref, qbuf.at[tile(0)], q_recv.at[0])
            own_q.start()
            clear()
            own_q.wait()
            key_landed(last * panels)
            score(jnp.int32(last), [0], 1)
            own = partial(0)
            result_landed(0)
            got[0] = merge(own, got[0])

        @pl.when(chip != 0)
        def _():
            result_landed(0)

        result_landed(1)
        merged_ref[...] = merge(got[0], got[1])

        @pl.when(spot != 0)
        def _():
            query_copy(mate, panels + core, 1).wait_send()

        key_copy(chip).wait_send()
        query_copy(chip, core, 0).wait_send()
        below(lambda copy: copy.wait_send())


def finish(merged_ref, matched_ref, energy_ref):
    top, total = merged_ref[:LEVELS], merged_ref[LEVELS : 2 * LEVELS]
    energy_ref[...] = top + jnp.log(total)
    matched_ref[:, 0, :] = merged_ref[2 * LEVELS : 3 * LEVELS] / total
    matched_ref[:, 1, :] = merged_ref[3 * LEVELS :] / total


def body(blk, panels, first_frame, second_frame):
    queries, channels = first_frame.shape
    _, rows, cols, _ = second_frame.shape
    keys = second_frame.reshape(rows * cols, channels)
    dma = pltpu.SemaphoreType.DMA
    merged = pl.pallas_call(
        functools.partial(kernel, (blk, panels, rows, cols)),
        out_shape=pltpu.VMEM((4 * LEVELS, queries), jnp.float32),
        in_specs=[pl.BlockSpec(memory_space=pl.ANY)] * 2,
        out_specs=pl.BlockSpec(memory_space=pltpu.VMEM),
        scratch_shapes=[
            pltpu.VMEM((2 * panels * queries, channels), jnp.bfloat16),
            pltpu.VMEM((blk * panels, rows * cols, channels), jnp.bfloat16),
            pltpu.VMEM((LEVELS, 4, cols, 2 * panels * queries), jnp.float32),
            pltpu.VMEM((2 * panels, 4 * LEVELS, queries), jnp.float32),
            pltpu.VMEM((2, 4 * LEVELS, queries), jnp.float32),
            pltpu.SemaphoreType.REGULAR((blk,)),
            dma((blk + 1,)), dma((blk * panels,)), dma((blk * panels,)),
            dma((panels,)), dma((2 * panels,)),
            dma((2 * panels,)), dma((2,)),
        ],
        compiler_params=pltpu.CompilerParams(collective_id=0, has_side_effects=True),
        name="corr",
    )(first_frame, keys)
    return pl.pallas_call(
        finish,
        out_shape=(jax.ShapeDtypeStruct((LEVELS, 2, queries), jnp.float32),
                   jax.ShapeDtypeStruct((LEVELS, queries), jnp.float32)),
        in_specs=[pl.BlockSpec(memory_space=pltpu.VMEM)],
        out_specs=(pl.BlockSpec(memory_space=pltpu.VMEM), pl.BlockSpec(memory_space=pltpu.VMEM)),
        name="finish",
    )(pltpu.with_memory_space_constraint(merged, pltpu.VMEM))


def solution(mesh):
    placed = (P(("pairs", "blk", "panel"), None), P(("pairs", "blk"), None, "panel", None))
    return jax.shard_map(
        functools.partial(body, mesh.shape["blk"], mesh.shape["panel"]),
        mesh=mesh,
        in_specs=placed,
        out_specs=(P(None, None, ("pairs", "blk", "panel")), P(None, ("pairs", "blk", "panel"))),
        check_vma=False,
    )
```

```python
import functools
import math

import jax
import jax.numpy as jnp
from jax import lax
from jax.experimental import pallas as pl
from jax.experimental.pallas import tpu as pltpu
from jax.sharding import PartitionSpec as P

LEVELS = 4
COLBLK = 8
BCOLS = 16
INNER = 2
NEG = -1e30
MESH = pl.DeviceIdType.MESH


def absorb(raw, sources, rows, cols, total_rows, total_cols, rates, state, lane):
    n = len(sources)
    q = raw.shape[-1]
    col = lax.broadcasted_iota(jnp.int32, (cols, q), 0)
    values = raw.reshape(n, rows, cols, q)
    for level in range(LEVELS):
        step = 2**level
        if level:
            pairs = values.reshape(n, rows // step, 2, cols, q)
            values = pairs[:, :, 0] + pairs[:, :, 1]
            values = values + pltpu.roll(values, step // 2, 2)
        height = rows // step
        old = state[level, 0, :, lane]
        top = jnp.maximum(old, jnp.max(values, axis=(0, 1)))
        weights = jnp.exp2((values - top) * rates[level])
        decay = jnp.exp2((old - top) * rates[level])
        col_in = ((col >> level).astype(jnp.float32) + 0.5) * (step / total_cols)
        total = state[level, 1, :, lane] * decay
        row_sum = state[level, 2, :, lane] * decay
        col_sum = state[level, 3, :, lane] * decay
        for s, (row_base, col_base) in enumerate(sources):
            part = weights[s, 0]
            part_row = weights[s, 0] * (0.5 * step / total_rows)
            for i in range(1, height):
                part = part + weights[s, i]
                part_row = part_row + weights[s, i] * ((i + 0.5) * step / total_rows)
            total = total + part
            row_sum = row_sum + (part_row + part * row_base)
            col_sum = col_sum + part * (col_in + col_base)
        state[level, 0, :, lane] = top
        state[level, 1, :, lane] = total
        state[level, 2, :, lane] = row_sum
        state[level, 3, :, lane] = col_sum


def settle(cols, rates, state, lane):
    tops, totals, row_sums, col_sums = [], [], [], []
    for level in range(LEVELS):
        step = 2**level
        top = state[level, 0, :, lane]
        col = lax.broadcasted_iota(jnp.int32, top.shape, 0)
        valid = (col & (step - 1)) == step - 1
        best = jnp.max(jnp.where(valid, top, NEG), axis=0, keepdims=True)
        scale = jnp.exp2((top - best) * rates[level])
        for rows_out, i in ((totals, 1), (row_sums, 2), (col_sums, 3)):
            term = jnp.where(valid, state[level, i, :, lane] * scale, 0.0)
            rows_out.append(jnp.sum(term, axis=0, keepdims=True))
        tops.append(best * (rates[level] * math.log(2.0)))
    return jnp.concatenate(tops + totals + row_sums + col_sums, axis=0)


def merge(one, two):
    top = jnp.maximum(one[:LEVELS], two[:LEVELS])
    one_scale, two_scale = jnp.exp(one[:LEVELS] - top), jnp.exp(two[:LEVELS] - top)
    sums = [one[LEVELS * i : LEVELS * (i + 1)] * one_scale + two[LEVELS * i : LEVELS * (i + 1)] * two_scale
            for i in (1, 2, 3)]
    return jnp.concatenate([top] + sums, axis=0)


def kernel(dims, q_ref, k_ref, merged_ref, qbuf, kbuf, state, done, got, ready,
           k_send, k_recv, q_send, q_recv, r_send, r_recv):
    blk, panels, rows, cols = dims
    outer = blk // INNER
    queries = q_ref.shape[0]
    keys = rows * cols
    total_rows, total_cols = rows * blk // COLBLK, BCOLS * COLBLK
    chip, core = lax.axis_index("blk"), lax.axis_index("panel")
    me = chip * panels + core
    hub = panels - 1
    line, spot = chip // INNER, chip % INNER
    mate = line * INNER + (INNER - 1 - spot)
    last = blk - 1
    barrier = pltpu.get_barrier_semaphore()
    rates = [3.0 / math.sqrt(k_ref.shape[-1]) / math.log(2.0) / 2**level for level in range(LEVELS)]

    def at(where, side):
        return {"blk": where, "panel": side}

    def each(low, high, step):
        lax.fori_loop(low, high, lambda i, _: (step(i), 0)[1], 0)

    def tile(i):
        return pl.ds(i * queries, queries)

    def tiles(half):
        return pl.ds(half * panels * queries, panels * queries)

    def key_copy(where, side=hub):
        apart = (chip == last) & (where == 0)
        return pltpu.make_async_remote_copy(
            k_ref, kbuf.at[me], k_send.at[jnp.where(apart, outer, where // INNER)],
            k_recv.at[jnp.where(apart, outer + hub - core, line)],
            device_id=at(where, side), device_id_type=MESH)

    def below(act):
        @pl.when(chip == last)
        def _():
            @pl.when(core != hub)
            def _():
                act(key_copy(0, 0))

            act(key_copy(0))

        def step(i):
            swap = (chip == last) & (i < 2)
            act(key_copy(jnp.where(swap, 1 - i, i) * INNER + spot))

        each(0, line, step)

    def below_sent():
        @pl.when(chip == last)
        def _():
            @pl.when(core != hub)
            def _():
                pltpu.make_async_copy(kbuf.at[:2], kbuf.at[:2], k_send.at[outer]).wait()

            @pl.when(core == hub)
            def _():
                key_copy(0).wait_send()

        each(0, line, lambda i: key_copy(i * INNER + spot).wait_send())

    def query_copy(where, place):
        return pltpu.make_async_remote_copy(
            q_ref, qbuf.at[tile(place)], q_send, q_recv.at[place // panels],
            device_id=at(where, hub), device_id_type=MESH)

    def pair(chip):
        return kbuf.at[pl.ds(chip * panels, panels)]

    def lift(where):
        return pltpu.make_async_remote_copy(
            pair(chip), pair(chip), k_send.at[where // INNER], k_recv.at[line],
            device_id=at(where, hub), device_id_type=MESH)

    def lend():
        return pltpu.make_async_remote_copy(
            qbuf.at[tiles(0)], qbuf.at[tiles(1)], q_send, q_recv.at[1],
            device_id=at(mate, hub), device_id_type=MESH)

    def result_copy(where, place, side):
        return pltpu.make_async_remote_copy(
            done.at[place * panels + side], got.at[place], r_send, r_recv,
            device_id=at(where, side), device_id_type=MESH)

    def keys_landed(source):
        pltpu.make_async_copy(pair(source), pair(source), k_recv.at[source // INNER]).wait()

    def late_landed(side):
        pltpu.make_async_copy(k_ref, kbuf.at[last * panels + side], k_recv.at[outer + hub - side]).wait()

    def queries_landed(half):
        pltpu.make_async_copy(qbuf.at[tiles(half)], qbuf.at[tiles(half)], q_recv.at[half]).wait()

    def score(source, sides, first, tiles):
        row_base = (source // COLBLK).astype(jnp.float32) * (rows / total_rows)
        left = (source % COLBLK) * BCOLS
        sources = [(row_base, (left + side * cols).astype(jnp.float32) * (1.0 / total_cols)) for side in sides]
        block = kbuf[pl.ds(source * panels + sides[0], len(sides))].reshape(len(sides) * keys, kbuf.shape[-1])
        raw = lax.dot_general(block, qbuf[first * queries : (first + tiles) * queries], (((1,), (1,)), ((), ())),
                              preferred_element_type=jnp.float32)
        for i in range(tiles):
            absorb(raw[:, i * queries : (i + 1) * queries], sources, rows, cols,
                   total_rows, total_cols, rates, state, tile(first + i))

    def clear():
        state[:, 0] = jnp.full_like(state[:, 0], NEG)
        state[:, 1:] = jnp.zeros_like(state[:, 1:])

    def partial(place):
        return settle(cols, rates, state, tile(place))

    greeted = line + jnp.where(spot != 0, 1, 0) + jnp.where(chip == last, panels, 0)

    @pl.when(core == hub)
    def _():
        own_k = pltpu.make_async_copy(k_ref, kbuf.at[me], k_recv.at[line])
        own_q = pltpu.make_async_copy(q_ref, qbuf.at[tile(hub)], q_recv.at[0])

        def greet(where):
            for side in range(panels):
                pl.semaphore_signal(barrier, inc=1, device_id=at(where, side), device_id_type=MESH)

        def answer(where):
            pl.semaphore_signal(ready.at[line], inc=1, device_id=at(where, hub), device_id_type=MESH)

        for side in range(hub):
            pl.semaphore_signal(barrier, inc=1, device_id=at(chip, side), device_id_type=MESH)

        @pl.when(spot == 0)
        def _():
            greet(mate)

        each(line + 1, outer, lambda i: greet(i * INNER + spot))

        @pl.when(chip == 0)
        def _():
            greet(last)

        @pl.when(chip != 0)
        def _():
            pl.semaphore_wait(barrier, greeted)

        below(lambda copy: copy.start())

        @pl.when(spot != 0)
        def _():
            query_copy(mate, panels + hub).start()
            answer(mate)

        each(0, line, lambda i: answer(i * INNER + spot))
        own_k.start()
        own_q.start()
        clear()
        queries_landed(0)

        @pl.when(spot == 0)
        def _():
            pl.semaphore_wait(ready.at[line], 1)
            lend().start()

        keys_landed(chip)

        def send_up(i):
            pl.semaphore_wait(ready.at[i], 1)
            lift(i * INNER + spot).start()

        each(line + 1, outer, send_up)
        queries_landed(1)

        def in_turn(turn):
            return jnp.where(turn <= line, line - turn, turn) * INNER + spot

        def take(turn):
            source = in_turn(turn)

            @pl.when(source != chip)
            def _():
                keys_landed(source)

            score(source, range(panels), 0, 2 * panels)

        turns = jnp.where(chip == 1, outer - 2, outer - 1)
        each(0, turns, take)
        final = in_turn(turns)
        keys_landed(final)
        score(final, range(panels), panels, panels)
        for side in range(panels):
            done[panels + side] = partial(panels + side)
            result_copy(mate, 1, side).start()
        score(final, range(panels), 0, panels)

        def return_rest():
            for side in range(hub):
                done[side] = partial(side)
                result_copy(chip, 0, side).start()

        @pl.when(chip == 0)
        def _():
            late_landed(hub)
            score(jnp.int32(last), [hub], 0, panels)
            return_rest()
            late_landed(0)
            score(jnp.int32(last), [0], hub, 1)

        @pl.when(chip == 1)
        def _():
            keys_landed(jnp.int32(last))
            score(jnp.int32(last), range(panels), 0, panels)

        @pl.when(chip != 0)
        def _():
            return_rest()

        own = partial(hub)
        pltpu.make_async_copy(done.at[0], got.at[1], r_recv).wait()
        merged_ref[...] = merge(own, got[1])
        sent = pl.ds(0, hub + panels)
        pltpu.make_async_copy(done.at[sent], done.at[sent], r_send).wait()

        @pl.when(spot == 0)
        def _():
            lend().wait_send()

        @pl.when(spot != 0)
        def _():
            query_copy(mate, panels + hub).wait_send()

        below_sent()
        each(line + 1, outer, lambda i: lift(i * INNER + spot).wait_send())

    @pl.when(core != hub)
    def _():
        @pl.when(chip == 0)
        def _():
            for side in range(panels):
                pl.semaphore_signal(barrier, inc=1, device_id=at(last, side), device_id_type=MESH)

        pl.semaphore_wait(barrier, greeted + 1)
        below(lambda copy: copy.start())

        @pl.when(spot != 0)
        def _():
            query_copy(mate, panels + core).start()

        query_copy(chip, core).start()
        key_copy(chip).start()

        @pl.when(chip == 0)
        def _():
            own_q = pltpu.make_async_copy(q_ref, qbuf.at[tile(0)], q_recv.at[0])
            own_q.start()
            clear()
            own_q.wait()
            late_landed(0)
            score(jnp.int32(last), [0], 0, 1)

        pltpu.make_async_copy(got, got, r_recv).wait()
        both = merge(got[0], got[1])

        @pl.when(chip == 0)
        def _():
            merged_ref[...] = merge(partial(0), both)

        @pl.when(chip != 0)
        def _():
            merged_ref[...] = both

        @pl.when(spot == 0)
        def _():
            query_copy(chip, core).wait_send()

        @pl.when(spot != 0)
        def _():
            pltpu.make_async_copy(qbuf.at[tiles(0)], qbuf.at[tiles(0)], q_send).wait()

        key_copy(chip).wait_send()
        below_sent()


def finish(merged_ref, matched_ref, energy_ref):
    top, total = merged_ref[:LEVELS], merged_ref[LEVELS : 2 * LEVELS]
    energy_ref[...] = top + jnp.log(total)
    matched_ref[:, 0, :] = merged_ref[2 * LEVELS : 3 * LEVELS] / total
    matched_ref[:, 1, :] = merged_ref[3 * LEVELS :] / total


def body(blk, panels, first_frame, second_frame):
    queries, channels = first_frame.shape
    _, rows, cols, _ = second_frame.shape
    keys = second_frame.reshape(rows * cols, channels)
    outer = blk // INNER
    dma = pltpu.SemaphoreType.DMA
    merged = pl.pallas_call(
        functools.partial(kernel, (blk, panels, rows, cols)),
        out_shape=pltpu.VMEM((4 * LEVELS, queries), jnp.float32),
        in_specs=[pl.BlockSpec(memory_space=pl.ANY)] * 2,
        out_specs=pl.BlockSpec(memory_space=pltpu.VMEM),
        scratch_shapes=[
            pltpu.VMEM((2 * panels * queries, channels), jnp.bfloat16),
            pltpu.VMEM((blk * panels, rows * cols, channels), jnp.bfloat16),
            pltpu.VMEM((LEVELS, 4, cols, 2 * panels * queries), jnp.float32),
            pltpu.VMEM((2 * panels, 4 * LEVELS, queries), jnp.float32),
            pltpu.VMEM((2, 4 * LEVELS, queries), jnp.float32),
            pltpu.SemaphoreType.REGULAR((outer,)),
            dma((outer + 1,)), dma((outer + panels,)),
            dma, dma((2,)), dma, dma,
        ],
        compiler_params=pltpu.CompilerParams(collective_id=0, has_side_effects=True),
        name="corr",
    )(first_frame, keys)
    return pl.pallas_call(
        finish,
        out_shape=(jax.ShapeDtypeStruct((LEVELS, 2, queries), jnp.float32),
                   jax.ShapeDtypeStruct((LEVELS, queries), jnp.float32)),
        in_specs=[pl.BlockSpec(memory_space=pltpu.VMEM)],
        out_specs=(pl.BlockSpec(memory_space=pltpu.VMEM), pl.BlockSpec(memory_space=pltpu.VMEM)),
        name="finish",
    )(pltpu.with_memory_space_constraint(merged, pltpu.VMEM))


def solution(mesh):
    placed = (P(("pairs", "blk", "panel"), None), P(("pairs", "blk"), None, "panel", None))
    return jax.shard_map(
        functools.partial(body, mesh.shape["blk"], mesh.shape["panel"]),
        mesh=mesh,
        in_specs=placed,
        out_specs=(P(None, None, ("pairs", "blk", "panel")), P(None, ("pairs", "blk", "panel"))),
        check_vma=False,
    )
```

```python
import functools
import math

import jax
import jax.numpy as jnp
from jax import lax
from jax.experimental import pallas as pl
from jax.experimental.pallas import tpu as pltpu
from jax.sharding import PartitionSpec as P

LEVELS = 4
COLBLK = 8
BCOLS = 16
INNER = 2
NEG = -1e30
MESH = pl.DeviceIdType.MESH


def absorb(raw, sources, rows, cols, total_rows, total_cols, rates, state, lane):
    n = len(sources)
    q = raw.shape[-1]
    col = lax.broadcasted_iota(jnp.int32, (cols, q), 0)
    values = raw.reshape(n, rows, cols, q)
    for level in range(LEVELS):
        step = 2**level
        if level:
            pairs = values.reshape(n, rows // step, 2, cols, q)
            values = pairs[:, :, 0] + pairs[:, :, 1]
            values = values + pltpu.roll(values, step // 2, 2)
        height = rows // step
        old = state[level, 0, :, lane]
        top = jnp.maximum(old, jnp.max(values, axis=(0, 1)))
        weights = jnp.exp2((values - top) * rates[level])
        decay = jnp.exp2((old - top) * rates[level])
        col_in = ((col >> level).astype(jnp.float32) + 0.5) * (step / total_cols)
        total = state[level, 1, :, lane] * decay
        row_sum = state[level, 2, :, lane] * decay
        col_sum = state[level, 3, :, lane] * decay
        for s, (row_base, col_base) in enumerate(sources):
            part = weights[s, 0]
            part_row = weights[s, 0] * (0.5 * step / total_rows)
            for i in range(1, height):
                part = part + weights[s, i]
                part_row = part_row + weights[s, i] * ((i + 0.5) * step / total_rows)
            total = total + part
            row_sum = row_sum + (part_row + part * row_base)
            col_sum = col_sum + part * (col_in + col_base)
        state[level, 0, :, lane] = top
        state[level, 1, :, lane] = total
        state[level, 2, :, lane] = row_sum
        state[level, 3, :, lane] = col_sum


def settle(cols, rates, state, lane):
    tops, totals, row_sums, col_sums = [], [], [], []
    for level in range(LEVELS):
        step = 2**level
        top = state[level, 0, :, lane]
        col = lax.broadcasted_iota(jnp.int32, top.shape, 0)
        valid = (col & (step - 1)) == step - 1
        best = jnp.max(jnp.where(valid, top, NEG), axis=0, keepdims=True)
        scale = jnp.exp2((top - best) * rates[level])
        for rows_out, i in ((totals, 1), (row_sums, 2), (col_sums, 3)):
            term = jnp.where(valid, state[level, i, :, lane] * scale, 0.0)
            rows_out.append(jnp.sum(term, axis=0, keepdims=True))
        tops.append(best * (rates[level] * math.log(2.0)))
    return jnp.concatenate(tops + totals + row_sums + col_sums, axis=0)


def merge(one, two):
    top = jnp.maximum(one[:LEVELS], two[:LEVELS])
    one_scale, two_scale = jnp.exp(one[:LEVELS] - top), jnp.exp(two[:LEVELS] - top)
    sums = [one[LEVELS * i : LEVELS * (i + 1)] * one_scale + two[LEVELS * i : LEVELS * (i + 1)] * two_scale
            for i in (1, 2, 3)]
    return jnp.concatenate([top] + sums, axis=0)


def kernel(dims, q_ref, k_ref, merged_ref, qbuf, kbuf, state, done, got, ready,
           k_send, k_recv, q_send, q_recv, r_send, r_recv):
    blk, panels, rows, cols = dims
    outer = blk // INNER
    queries = q_ref.shape[0]
    keys = rows * cols
    total_rows, total_cols = rows * blk // COLBLK, BCOLS * COLBLK
    chip, core = lax.axis_index("blk"), lax.axis_index("panel")
    me = chip * panels + core
    hub = panels - 1
    line, spot = chip // INNER, chip % INNER
    mate = line * INNER + (INNER - 1 - spot)
    last = blk - 1
    lowest = jnp.where((chip == last) & (core == hub), 1, 0)
    whole_line = (chip == last) & (core != hub)
    barrier = pltpu.get_barrier_semaphore()
    rates = [3.0 / math.sqrt(k_ref.shape[-1]) / math.log(2.0) / 2**level for level in range(LEVELS)]

    def at(where, side):
        return {"blk": where, "panel": side}

    def each(low, high, step):
        lax.fori_loop(low, high, lambda i, _: (step(i), 0)[1], 0)

    def tile(i):
        return pl.ds(i * queries, queries)

    def tiles(half):
        return pl.ds(half * panels * queries, panels * queries)

    def key_copy(where, side=hub):
        apart = (chip == last) & (where == 0)
        return pltpu.make_async_remote_copy(
            k_ref, kbuf.at[me], k_send.at[jnp.where(apart, outer, where // INNER)],
            k_recv.at[jnp.where(apart, outer + hub - core, line)],
            device_id=at(where, side), device_id_type=MESH)

    def below(act):
        @pl.when(chip == last)
        def _():
            @pl.when(core != hub)
            def _():
                act(key_copy(0, 0))

            act(key_copy(0))

        def step(i):
            swap = whole_line & (i < 2)
            act(key_copy(jnp.where(swap, 1 - i, i) * INNER + spot))

        each(lowest, line, step)

    def below_sent():
        @pl.when(chip == last)
        def _():
            @pl.when(core != hub)
            def _():
                pltpu.make_async_copy(kbuf.at[:2], kbuf.at[:2], k_send.at[outer]).wait()

            @pl.when(core == hub)
            def _():
                key_copy(0).wait_send()

        each(lowest, line, lambda i: key_copy(i * INNER + spot).wait_send())

    def query_copy(where, place):
        return pltpu.make_async_remote_copy(
            q_ref, qbuf.at[tile(place)], q_send, q_recv.at[place // panels],
            device_id=at(where, hub), device_id_type=MESH)

    def pair(chip):
        return kbuf.at[pl.ds(chip * panels, panels)]

    def lift(where):
        return pltpu.make_async_remote_copy(
            pair(chip), pair(chip), k_send.at[where // INNER], k_recv.at[line],
            device_id=at(where, hub), device_id_type=MESH)

    def lend():
        return pltpu.make_async_remote_copy(
            qbuf.at[tiles(0)], qbuf.at[tiles(1)], q_send, q_recv.at[1],
            device_id=at(mate, hub), device_id_type=MESH)

    def result_copy(where, place, side):
        return pltpu.make_async_remote_copy(
            done.at[place * panels + side], got.at[place], r_send, r_recv,
            device_id=at(where, side), device_id_type=MESH)

    def keys_landed(source):
        pltpu.make_async_copy(pair(source), pair(source), k_recv.at[source // INNER]).wait()

    def late_landed(side):
        pltpu.make_async_copy(k_ref, kbuf.at[last * panels + side], k_recv.at[outer + hub - side]).wait()

    def queries_landed(half):
        pltpu.make_async_copy(qbuf.at[tiles(half)], qbuf.at[tiles(half)], q_recv.at[half]).wait()

    def score(source, sides, first, tiles):
        row_base = (source // COLBLK).astype(jnp.float32) * (rows / total_rows)
        left = (source % COLBLK) * BCOLS
        sources = [(row_base, (left + side * cols).astype(jnp.float32) * (1.0 / total_cols)) for side in sides]
        block = kbuf[pl.ds(source * panels + sides[0], len(sides))].reshape(len(sides) * keys, kbuf.shape[-1])
        raw = lax.dot_general(block, qbuf[first * queries : (first + tiles) * queries], (((1,), (1,)), ((), ())),
                              preferred_element_type=jnp.float32)
        for i in range(tiles):
            absorb(raw[:, i * queries : (i + 1) * queries], sources, rows, cols,
                   total_rows, total_cols, rates, state, tile(first + i))

    def clear():
        state[:, 0] = jnp.full_like(state[:, 0], NEG)
        state[:, 1:] = jnp.zeros_like(state[:, 1:])

    def partial(place):
        return settle(cols, rates, state, tile(place))

    greeted = line + jnp.where(spot != 0, 1, 0) + jnp.where(chip == last, panels, 0)

    @pl.when(core == hub)
    def _():
        own_k = pltpu.make_async_copy(k_ref, kbuf.at[me], k_recv.at[line])
        own_q = pltpu.make_async_copy(q_ref, qbuf.at[tile(hub)], q_recv.at[0])

        def greet(where):
            for side in range(panels):
                pl.semaphore_signal(barrier, inc=1, device_id=at(where, side), device_id_type=MESH)

        def answer(where):
            pl.semaphore_signal(ready.at[line], inc=1, device_id=at(where, hub), device_id_type=MESH)

        for side in range(hub):
            pl.semaphore_signal(barrier, inc=1, device_id=at(chip, side), device_id_type=MESH)

        @pl.when(spot == 0)
        def _():
            greet(mate)

        each(line + 1, outer, lambda i: greet(i * INNER + spot))

        @pl.when(chip == 0)
        def _():
            greet(last)

        @pl.when(chip != 0)
        def _():
            pl.semaphore_wait(barrier, greeted)

        below(lambda copy: copy.start())

        @pl.when(spot != 0)
        def _():
            query_copy(mate, panels + hub).start()
            answer(mate)

        each(0, line, lambda i: answer(i * INNER + spot))
        own_k.start()
        own_q.start()
        clear()
        queries_landed(0)

        @pl.when(spot == 0)
        def _():
            pl.semaphore_wait(ready.at[line], 1)
            lend().start()

        keys_landed(chip)

        def send_up(i):
            pl.semaphore_wait(ready.at[i], 1)
            lift(i * INNER + spot).start()

        each(line + 1, outer, send_up)
        queries_landed(1)

        def in_turn(turn):
            return jnp.where(turn <= line, line - turn, turn) * INNER + spot

        def take(turn):
            source = in_turn(turn)

            @pl.when(source != chip)
            def _():
                keys_landed(source)

            score(source, range(panels), 0, 2 * panels)

        def return_pair():
            for side in range(panels):
                done[panels + side] = partial(panels + side)
                result_copy(mate, 1, side).start()

        def return_rest():
            for side in range(hub):
                done[side] = partial(side)
                result_copy(chip, 0, side).start()

        turns = jnp.where(chip == 1, outer - 2, outer - 1)
        each(0, turns, take)
        final = in_turn(turns)
        keys_landed(final)
        score(final, range(panels), panels, panels)

        @pl.when(chip != 0)
        def _():
            return_pair()

        score(final, range(panels), 0, panels)

        @pl.when(chip == 0)
        def _():
            late_landed(hub)
            score(jnp.int32(last), [hub], 0, 2 * panels)
            return_pair()
            return_rest()
            late_landed(0)
            score(jnp.int32(last), [0], hub, 1)

        @pl.when(chip == 1)
        def _():
            pltpu.make_async_copy(k_ref, kbuf.at[last * panels], k_recv.at[outer - 1]).wait()
            score(jnp.int32(last), [0], 0, panels)

        @pl.when(chip != 0)
        def _():
            return_rest()

        own = partial(hub)
        pltpu.make_async_copy(done.at[0], got.at[1], r_recv).wait()
        merged_ref[...] = merge(own, got[1])
        sent = pl.ds(0, hub + panels)
        pltpu.make_async_copy(done.at[sent], done.at[sent], r_send).wait()

        @pl.when(spot == 0)
        def _():
            lend().wait_send()

        @pl.when(spot != 0)
        def _():
            query_copy(mate, panels + hub).wait_send()

        below_sent()
        each(line + 1, outer, lambda i: lift(i * INNER + spot).wait_send())

    @pl.when(core != hub)
    def _():
        @pl.when(chip == 0)
        def _():
            for side in range(panels):
                pl.semaphore_signal(barrier, inc=1, device_id=at(last, side), device_id_type=MESH)

        pl.semaphore_wait(barrier, greeted + 1)
        below(lambda copy: copy.start())

        @pl.when(spot != 0)
        def _():
            query_copy(mate, panels + core).start()

        query_copy(chip, core).start()
        key_copy(chip).start()

        @pl.when(chip == 0)
        def _():
            own_q = pltpu.make_async_copy(q_ref, qbuf.at[tile(0)], q_recv.at[0])
            own_q.start()
            clear()
            own_q.wait()
            late_landed(0)
            score(jnp.int32(last), [0], 0, 1)

        pltpu.make_async_copy(got, got, r_recv).wait()
        both = merge(got[0], got[1])

        @pl.when(chip == 0)
        def _():
            merged_ref[...] = merge(partial(0), both)

        @pl.when(chip != 0)
        def _():
            merged_ref[...] = both

        @pl.when(spot == 0)
        def _():
            query_copy(chip, core).wait_send()

        @pl.when(spot != 0)
        def _():
            pltpu.make_async_copy(qbuf.at[tiles(0)], qbuf.at[tiles(0)], q_send).wait()

        key_copy(chip).wait_send()
        below_sent()


def finish(merged_ref, matched_ref, energy_ref):
    top, total = merged_ref[:LEVELS], merged_ref[LEVELS : 2 * LEVELS]
    energy_ref[...] = top + jnp.log(total)
    matched_ref[:, 0, :] = merged_ref[2 * LEVELS : 3 * LEVELS] / total
    matched_ref[:, 1, :] = merged_ref[3 * LEVELS :] / total


def body(blk, panels, first_frame, second_frame):
    queries, channels = first_frame.shape
    _, rows, cols, _ = second_frame.shape
    keys = second_frame.reshape(rows * cols, channels)
    outer = blk // INNER
    dma = pltpu.SemaphoreType.DMA
    merged = pl.pallas_call(
        functools.partial(kernel, (blk, panels, rows, cols)),
        out_shape=pltpu.VMEM((4 * LEVELS, queries), jnp.float32),
        in_specs=[pl.BlockSpec(memory_space=pl.ANY)] * 2,
        out_specs=pl.BlockSpec(memory_space=pltpu.VMEM),
        scratch_shapes=[
            pltpu.VMEM((2 * panels * queries, channels), jnp.bfloat16),
            pltpu.VMEM((blk * panels, rows * cols, channels), jnp.bfloat16),
            pltpu.VMEM((LEVELS, 4, cols, 2 * panels * queries), jnp.float32),
            pltpu.VMEM((2 * panels, 4 * LEVELS, queries), jnp.float32),
            pltpu.VMEM((2, 4 * LEVELS, queries), jnp.float32),
            pltpu.SemaphoreType.REGULAR((outer,)),
            dma((outer + 1,)), dma((outer + panels,)),
            dma, dma((2,)), dma, dma,
        ],
        compiler_params=pltpu.CompilerParams(collective_id=0, has_side_effects=True),
        name="corr",
    )(first_frame, keys)
    return pl.pallas_call(
        finish,
        out_shape=(jax.ShapeDtypeStruct((LEVELS, 2, queries), jnp.float32),
                   jax.ShapeDtypeStruct((LEVELS, queries), jnp.float32)),
        in_specs=[pl.BlockSpec(memory_space=pltpu.VMEM)],
        out_specs=(pl.BlockSpec(memory_space=pltpu.VMEM), pl.BlockSpec(memory_space=pltpu.VMEM)),
        name="finish",
    )(pltpu.with_memory_space_constraint(merged, pltpu.VMEM))


def solution(mesh):
    placed = (P(("pairs", "blk", "panel"), None), P(("pairs", "blk"), None, "panel", None))
    return jax.shard_map(
        functools.partial(body, mesh.shape["blk"], mesh.shape["panel"]),
        mesh=mesh,
        in_specs=placed,
        out_specs=(P(None, None, ("pairs", "blk", "panel")), P(None, ("pairs", "blk", "panel"))),
        check_vma=False,
    )
```

```python
import functools
import math

import jax
import jax.numpy as jnp
from jax import lax
from jax.experimental import pallas as pl
from jax.experimental.pallas import tpu as pltpu
from jax.sharding import PartitionSpec as P

LEVELS = 4
COLBLK = 8
BCOLS = 16
INNER = 2
NEG = -1e30
MESH = pl.DeviceIdType.MESH


def absorb(raw, sources, rows, cols, total_rows, total_cols, rates, state, lane):
    n = len(sources)
    q = raw.shape[-1]
    col = lax.broadcasted_iota(jnp.int32, (cols, q), 0)
    values = raw.reshape(n, rows, cols, q)
    for level in range(LEVELS):
        step = 2**level
        if level:
            pairs = values.reshape(n, rows // step, 2, cols, q)
            values = pairs[:, :, 0] + pairs[:, :, 1]
            values = values + pltpu.roll(values, step // 2, 2)
        height = rows // step
        old = state[level, 0, :, lane]
        top = jnp.maximum(old, jnp.max(values, axis=(0, 1)))
        weights = jnp.exp2((values - top) * rates[level])
        decay = jnp.exp2((old - top) * rates[level])
        col_in = ((col >> level).astype(jnp.float32) + 0.5) * (step / total_cols)
        total = state[level, 1, :, lane] * decay
        row_sum = state[level, 2, :, lane] * decay
        col_sum = state[level, 3, :, lane] * decay
        for s, (row_base, col_base) in enumerate(sources):
            part = weights[s, 0]
            part_row = weights[s, 0] * (0.5 * step / total_rows)
            for i in range(1, height):
                part = part + weights[s, i]
                part_row = part_row + weights[s, i] * ((i + 0.5) * step / total_rows)
            total = total + part
            row_sum = row_sum + (part_row + part * row_base)
            col_sum = col_sum + part * (col_in + col_base)
        state[level, 0, :, lane] = top
        state[level, 1, :, lane] = total
        state[level, 2, :, lane] = row_sum
        state[level, 3, :, lane] = col_sum


def settle(cols, rates, state, lane):
    tops, totals, row_sums, col_sums = [], [], [], []
    for level in range(LEVELS):
        step = 2**level
        top = state[level, 0, :, lane]
        col = lax.broadcasted_iota(jnp.int32, top.shape, 0)
        valid = (col & (step - 1)) == step - 1
        best = jnp.max(jnp.where(valid, top, NEG), axis=0, keepdims=True)
        scale = jnp.exp2((top - best) * rates[level])
        for rows_out, i in ((totals, 1), (row_sums, 2), (col_sums, 3)):
            term = jnp.where(valid, state[level, i, :, lane] * scale, 0.0)
            rows_out.append(jnp.sum(term, axis=0, keepdims=True))
        tops.append(best * (rates[level] * math.log(2.0)))
    return jnp.concatenate(tops + totals + row_sums + col_sums, axis=0)


def merge(one, two):
    top = jnp.maximum(one[:LEVELS], two[:LEVELS])
    one_scale, two_scale = jnp.exp(one[:LEVELS] - top), jnp.exp(two[:LEVELS] - top)
    sums = [one[LEVELS * i : LEVELS * (i + 1)] * one_scale + two[LEVELS * i : LEVELS * (i + 1)] * two_scale
            for i in (1, 2, 3)]
    return jnp.concatenate([top] + sums, axis=0)


def kernel(dims, q_ref, k_ref, merged_ref, qbuf, turned, kbuf, state, done, got, ready,
           send, k_recv, q_recv, r_send, r_recv):
    blk, panels, rows, cols = dims
    outer = blk // INNER
    queries = q_ref.shape[0]
    keys = rows * cols
    query_slots = queries // keys
    total_rows, total_cols = rows * blk // COLBLK, BCOLS * COLBLK
    chip, core = lax.axis_index("blk"), lax.axis_index("panel")
    me = chip * panels + core
    hub = panels - 1
    line, spot = chip // INNER, chip % INNER
    mate = line * INNER + (INNER - 1 - spot)
    last = blk - 1
    lowest = jnp.where((chip == last) & (core == hub), 1, 0)
    whole_line = (chip == last) & (core != hub)
    first_part = lax.axis_index("pairs") == 0
    barrier = pltpu.get_barrier_semaphore()
    rates = [3.0 / math.sqrt(k_ref.shape[-1]) / math.log(2.0) / 2**level for level in range(LEVELS)]

    def at(where, side):
        return {"blk": where, "panel": side}

    def each(low, high, step):
        lax.fori_loop(low, high, lambda i, _: (step(i), 0)[1], 0)

    def tile(i):
        return pl.ds(i * queries, queries)

    def tiles(half):
        return pl.ds(half * panels * queries, panels * queries)

    def key_copy(where, side=hub):
        apart = (chip == last) & (where == 0)
        return pltpu.make_async_remote_copy(
            k_ref, kbuf.at[me], send,
            k_recv.at[jnp.where(apart, outer + hub - core, line)],
            device_id=at(where, side), device_id_type=MESH)

    def below(act):
        @pl.when(whole_line)
        def _():
            act(key_copy(0, 0))

            @pl.when(first_part)
            def _():
                act(key_copy(0))

            act(key_copy(INNER + spot))

            @pl.when(jnp.logical_not(first_part))
            def _():
                act(key_copy(0))

            act(key_copy(spot))
            each(2, line, lambda i: act(key_copy(i * INNER + spot)))

        @pl.when((chip == last) & (core == hub))
        def _():
            act(key_copy(0))
            each(2, line, lambda i: act(key_copy(i * INNER + spot)))
            act(key_copy(INNER + spot))

        @pl.when(chip != last)
        def _():
            each(0, line, lambda i: act(key_copy(i * INNER + spot)))

    def all_sent(slots):
        for count in range(1, 2 * outer + 5):
            @pl.when(slots == count)
            def _():
                pltpu.make_async_copy(kbuf.at[:count], kbuf.at[:count], send).wait()

    def query_copy(where, place):
        return pltpu.make_async_remote_copy(
            q_ref, qbuf.at[tile(place)], send, q_recv.at[place // panels],
            device_id=at(where, hub), device_id_type=MESH)

    def pair(chip):
        return kbuf.at[pl.ds(chip * panels, panels)]

    def lift(where):
        return pltpu.make_async_remote_copy(
            pair(chip), pair(chip), send, k_recv.at[line],
            device_id=at(where, hub), device_id_type=MESH)

    def lend():
        return pltpu.make_async_remote_copy(
            qbuf.at[tiles(0)], qbuf.at[tiles(1)], send, q_recv.at[1],
            device_id=at(mate, hub), device_id_type=MESH)

    def result_copy(where, place, side):
        return pltpu.make_async_remote_copy(
            done.at[place * panels + side], got.at[place], r_send, r_recv,
            device_id=at(where, side), device_id_type=MESH)

    def keys_landed(source):
        pltpu.make_async_copy(pair(source), pair(source), k_recv.at[source // INNER]).wait()

    def late_landed(side):
        pltpu.make_async_copy(k_ref, kbuf.at[last * panels + side], k_recv.at[outer + hub - side]).wait()

    def queries_landed(half):
        pltpu.make_async_copy(qbuf.at[tiles(half)], qbuf.at[tiles(half)], q_recv.at[half]).wait()

    def score(source, sides, first, tiles):
        row_base = (source // COLBLK).astype(jnp.float32) * (rows / total_rows)
        left = (source % COLBLK) * BCOLS
        sources = [(row_base, (left + side * cols).astype(jnp.float32) * (1.0 / total_cols)) for side in sides]
        block = kbuf[pl.ds(source * panels + sides[0], len(sides))].reshape(len(sides) * keys, kbuf.shape[-1])
        raw = jnp.dot(block, turned[:, first * queries : (first + tiles) * queries],
                      preferred_element_type=jnp.float32)
        for i in range(tiles):
            absorb(raw[:, i * queries : (i + 1) * queries], sources, rows, cols,
                   total_rows, total_cols, rates, state, tile(first + i))

    def turn_queries(place, count):
        rows_in = pl.ds(place * queries, count * queries)
        turned[:, place * queries : (place + count) * queries] = qbuf[rows_in].T

    def clear():
        state[:, 0] = jnp.full_like(state[:, 0], NEG)
        state[:, 1:] = jnp.zeros_like(state[:, 1:])

    def partial(place):
        return settle(cols, rates, state, tile(place))

    greeted = line + jnp.where(spot != 0, 1, 0) + jnp.where(chip == last, panels, 0)

    @pl.when(core == hub)
    def _():
        own_k = pltpu.make_async_copy(k_ref, kbuf.at[me], k_recv.at[line])
        own_q = pltpu.make_async_copy(q_ref, qbuf.at[tile(hub)], q_recv.at[0])

        def greet(where):
            for side in reversed(range(panels)):
                pl.semaphore_signal(barrier, inc=1, device_id=at(where, side), device_id_type=MESH)

        def answer(where):
            pl.semaphore_signal(ready.at[line], inc=1, device_id=at(where, hub), device_id_type=MESH)

        @pl.when(spot == 0)
        def _():
            greet(mate)

        for side in range(hub):
            pl.semaphore_signal(barrier, inc=1, device_id=at(chip, side), device_id_type=MESH)

        each(line + 1, outer, lambda i: greet(i * INNER + spot))

        @pl.when(chip == 0)
        def _():
            greet(last)

        @pl.when(chip != 0)
        def _():
            pl.semaphore_wait(barrier, greeted)

        each(0, line, lambda i: answer(i * INNER + spot))
        below(lambda copy: copy.start())

        @pl.when(spot != 0)
        def _():
            answer(mate)
            query_copy(mate, panels + hub).start()

        own_k.start()
        own_q.start()
        clear()
        queries_landed(0)

        @pl.when(spot == 0)
        def _():
            pl.semaphore_wait(ready.at[line], 1)
            lend().start()

        turn_queries(0, panels)
        keys_landed(chip)

        def send_up(i):
            pl.semaphore_wait(ready.at[i], 1)
            lift(i * INNER + spot).start()

        each(line + 1, outer, send_up)
        queries_landed(1)
        turn_queries(panels, panels)

        def in_turn(turn):
            return jnp.where(turn <= line, line - turn, turn) * INNER + spot

        def take(turn):
            source = in_turn(turn)

            @pl.when(source != chip)
            def _():
                keys_landed(source)

            score(source, range(panels), 0, 2 * panels)

        def return_pair():
            for side in range(panels):
                done[panels + side] = partial(panels + side)
                result_copy(mate, 1, side).start()

        def return_rest():
            for side in range(hub):
                done[side] = partial(side)
                result_copy(chip, 0, side).start()

        turns = jnp.where(chip == 1, outer - 2, outer - 1)
        each(0, turns, take)
        final = in_turn(turns)
        keys_landed(final)
        score(final, range(panels), panels, panels)

        @pl.when(chip != 0)
        def _():
            return_pair()

        score(final, range(panels), 0, panels)

        @pl.when(chip == 0)
        def _():
            late_landed(hub)
            score(jnp.int32(last), [hub], 0, 2 * panels)
            return_pair()
            return_rest()
            late_landed(0)
            score(jnp.int32(last), [0], hub, 1)

        @pl.when(chip == 1)
        def _():
            pltpu.make_async_copy(k_ref, kbuf.at[last * panels], k_recv.at[outer - 1]).wait()
            score(jnp.int32(last), [0], 0, panels)

        @pl.when(chip != 0)
        def _():
            return_rest()

        own = partial(hub)

        all_sent(line - lowest + jnp.where(chip == last, 1, 0) + panels * (outer - 1 - line)
                 + query_slots * jnp.where(spot == 0, panels, 1))
        sent = pl.ds(0, hub + panels)
        pltpu.make_async_copy(done.at[sent], done.at[sent], r_send).wait()
        pltpu.make_async_copy(done.at[0], got.at[1], r_recv).wait()
        merged_ref[...] = merge(own, got[1])

    @pl.when(core != hub)
    def _():
        @pl.when(chip == 0)
        def _():
            for side in range(panels):
                pl.semaphore_signal(barrier, inc=1, device_id=at(last, side), device_id_type=MESH)

        pl.semaphore_wait(barrier, greeted + 1)
        below(lambda copy: copy.start())

        @pl.when(spot != 0)
        def _():
            query_copy(mate, panels + core).start()

        query_copy(chip, core).start()
        key_copy(chip).start()

        @pl.when(chip == 0)
        def _():
            own_q = pltpu.make_async_copy(q_ref, qbuf.at[tile(0)], q_recv.at[0])
            own_q.start()
            clear()
            own_q.wait()
            turn_queries(0, 1)
            late_landed(0)
            score(jnp.int32(last), [0], 0, 1)

        all_sent(line + jnp.where(chip == last, 2, 0) + 1 + query_slots * jnp.where(spot == 0, 1, 2))
        pltpu.make_async_copy(got, got, r_recv).wait()
        both = merge(got[0], got[1])

        @pl.when(chip == 0)
        def _():
            merged_ref[...] = merge(partial(0), both)

        @pl.when(chip != 0)
        def _():
            merged_ref[...] = both


def finish(merged_ref, matched_ref, energy_ref):
    top, total = merged_ref[:LEVELS], merged_ref[LEVELS : 2 * LEVELS]
    energy_ref[...] = top + jnp.log(total)
    matched_ref[:, 0, :] = merged_ref[2 * LEVELS : 3 * LEVELS] / total
    matched_ref[:, 1, :] = merged_ref[3 * LEVELS :] / total


def body(blk, panels, first_frame, second_frame):
    queries, channels = first_frame.shape
    _, rows, cols, _ = second_frame.shape
    keys = second_frame.reshape(rows * cols, channels)
    outer = blk // INNER
    dma = pltpu.SemaphoreType.DMA
    merged = pl.pallas_call(
        functools.partial(kernel, (blk, panels, rows, cols)),
        out_shape=pltpu.VMEM((4 * LEVELS, queries), jnp.float32),
        in_specs=[pl.BlockSpec(memory_space=pl.ANY)] * 2,
        out_specs=pl.BlockSpec(memory_space=pltpu.VMEM),
        scratch_shapes=[
            pltpu.VMEM((2 * panels * queries, channels), jnp.bfloat16),
            pltpu.VMEM((channels, 2 * panels * queries), jnp.bfloat16),
            pltpu.VMEM((blk * panels, rows * cols, channels), jnp.bfloat16),
            pltpu.VMEM((LEVELS, 4, cols, 2 * panels * queries), jnp.float32),
            pltpu.VMEM((2 * panels, 4 * LEVELS, queries), jnp.float32),
            pltpu.VMEM((2, 4 * LEVELS, queries), jnp.float32),
            pltpu.SemaphoreType.REGULAR((outer,)),
            dma, dma((outer + panels,)), dma((2,)), dma, dma,
        ],
        compiler_params=pltpu.CompilerParams(collective_id=0, has_side_effects=True),
        name="corr",
    )(first_frame, keys)
    return pl.pallas_call(
        finish,
        out_shape=(jax.ShapeDtypeStruct((LEVELS, 2, queries), jnp.float32),
                   jax.ShapeDtypeStruct((LEVELS, queries), jnp.float32)),
        in_specs=[pl.BlockSpec(memory_space=pltpu.VMEM)],
        out_specs=(pl.BlockSpec(memory_space=pltpu.VMEM), pl.BlockSpec(memory_space=pltpu.VMEM)),
        name="finish",
    )(pltpu.with_memory_space_constraint(merged, pltpu.VMEM))


def solution(mesh):
    placed = (P(("pairs", "blk", "panel"), None), P(("pairs", "blk"), None, "panel", None))
    return jax.shard_map(
        functools.partial(body, mesh.shape["blk"], mesh.shape["panel"]),
        mesh=mesh,
        in_specs=placed,
        out_specs=(P(None, None, ("pairs", "blk", "panel")), P(None, ("pairs", "blk", "panel"))),
        check_vma=False,
    )
```

```python
import functools
import math

import jax
import jax.numpy as jnp
from jax import lax
from jax.experimental import pallas as pl
from jax.experimental.pallas import tpu as pltpu
from jax.sharding import PartitionSpec as P

LEVELS = 4
COLBLK = 8
BCOLS = 16
INNER = 2
NEG = -1e30
MESH = pl.DeviceIdType.MESH


def absorb(raw, sources, rows, cols, total_rows, total_cols, rates, state, lane):
    n = len(sources)
    q = raw.shape[-1]
    col = lax.broadcasted_iota(jnp.int32, (cols, q), 0)
    values = raw.reshape(n, rows, cols, q)
    for level in range(LEVELS):
        step = 2**level
        if level:
            pairs = values.reshape(n, rows // step, 2, cols, q)
            values = pairs[:, :, 0] + pairs[:, :, 1]
            values = values + pltpu.roll(values, step // 2, 2)
        height = rows // step
        old = state[level, 0, :, lane]
        top = jnp.maximum(old, jnp.max(values, axis=(0, 1)))
        weights = jnp.exp2((values - top) * rates[level])
        decay = jnp.exp2((old - top) * rates[level])
        col_in = ((col >> level).astype(jnp.float32) + 0.5) * (step / total_cols)
        total = state[level, 1, :, lane] * decay
        row_sum = state[level, 2, :, lane] * decay
        col_sum = state[level, 3, :, lane] * decay
        for s, (row_base, col_base) in enumerate(sources):
            part = weights[s, 0]
            part_row = weights[s, 0] * (0.5 * step / total_rows)
            for i in range(1, height):
                part = part + weights[s, i]
                part_row = part_row + weights[s, i] * ((i + 0.5) * step / total_rows)
            total = total + part
            row_sum = row_sum + (part_row + part * row_base)
            col_sum = col_sum + part * (col_in + col_base)
        state[level, 0, :, lane] = top
        state[level, 1, :, lane] = total
        state[level, 2, :, lane] = row_sum
        state[level, 3, :, lane] = col_sum


def settle(cols, rates, state, lane):
    tops, totals, row_sums, col_sums = [], [], [], []
    for level in range(LEVELS):
        step = 2**level
        top = state[level, 0, :, lane]
        col = lax.broadcasted_iota(jnp.int32, top.shape, 0)
        valid = (col & (step - 1)) == step - 1
        best = jnp.max(jnp.where(valid, top, NEG), axis=0, keepdims=True)
        scale = jnp.exp2((top - best) * rates[level])
        for rows_out, i in ((totals, 1), (row_sums, 2), (col_sums, 3)):
            term = jnp.where(valid, state[level, i, :, lane] * scale, 0.0)
            rows_out.append(jnp.sum(term, axis=0, keepdims=True))
        tops.append(best * (rates[level] * math.log(2.0)))
    return jnp.concatenate(tops + totals + row_sums + col_sums, axis=0)


def merge(one, two):
    top = jnp.maximum(one[:LEVELS], two[:LEVELS])
    one_scale, two_scale = jnp.exp(one[:LEVELS] - top), jnp.exp(two[:LEVELS] - top)
    sums = [one[LEVELS * i : LEVELS * (i + 1)] * one_scale + two[LEVELS * i : LEVELS * (i + 1)] * two_scale
            for i in (1, 2, 3)]
    return jnp.concatenate([top] + sums, axis=0)


def kernel(dims, q_ref, k_ref, merged_ref, qbuf, turned, kbuf, state, done, got, ready,
           send, k_recv, q_recv, r_send, r_recv):
    blk, panels, rows, cols = dims
    outer = blk // INNER
    queries = q_ref.shape[0]
    keys = rows * cols
    query_slots = queries // keys
    total_rows, total_cols = rows * blk // COLBLK, BCOLS * COLBLK
    chip, core = lax.axis_index("blk"), lax.axis_index("panel")
    me = chip * panels + core
    hub = panels - 1
    line, spot = chip // INNER, chip % INNER
    mate = line * INNER + (INNER - 1 - spot)
    last = blk - 1
    lowest = jnp.where((chip == last) & (core == hub), 1, 0)
    whole_line = (chip == last) & (core != hub)
    first_part = lax.axis_index("pairs") == 0
    barrier = pltpu.get_barrier_semaphore()
    rates = [3.0 / math.sqrt(k_ref.shape[-1]) / math.log(2.0) / 2**level for level in range(LEVELS)]

    def at(where, side):
        return {"blk": where, "panel": side}

    def each(low, high, step):
        lax.fori_loop(low, high, lambda i, _: (step(i), 0)[1], 0)

    def tile(i):
        return pl.ds(pl.multiple_of(i * queries, queries), queries)

    def tiles(half):
        return pl.ds(half * panels * queries, panels * queries)

    def key_copy(where, side=hub):
        apart = (chip == last) & (where == 0)
        return pltpu.make_async_remote_copy(
            k_ref, kbuf.at[me], send,
            k_recv.at[jnp.where(apart, outer + hub - core, line)],
            device_id=at(where, side), device_id_type=MESH)

    def below(act):
        @pl.when(whole_line)
        def _():
            act(key_copy(0, 0))

            @pl.when(first_part)
            def _():
                act(key_copy(0))

            act(key_copy(INNER + spot))

            @pl.when(jnp.logical_not(first_part))
            def _():
                act(key_copy(0))

            act(key_copy(spot))
            each(2, line, lambda i: act(key_copy(i * INNER + spot)))

        @pl.when((chip == last) & (core == hub))
        def _():
            act(key_copy(0))
            each(2, line, lambda i: act(key_copy(i * INNER + spot)))
            act(key_copy(INNER + spot))

        @pl.when(chip != last)
        def _():
            each(0, line, lambda i: act(key_copy(i * INNER + spot)))

    def all_sent(slots):
        for count in range(1, 2 * outer + 5):
            @pl.when(slots == count)
            def _():
                pltpu.make_async_copy(kbuf.at[:count], kbuf.at[:count], send).wait()

    def query_copy(where, place):
        return pltpu.make_async_remote_copy(
            q_ref, qbuf.at[tile(place)], send, q_recv.at[place // panels],
            device_id=at(where, hub), device_id_type=MESH)

    def pair(chip):
        return kbuf.at[pl.ds(chip * panels, panels)]

    def lift(where):
        return pltpu.make_async_remote_copy(
            pair(chip), pair(chip), send, k_recv.at[line],
            device_id=at(where, hub), device_id_type=MESH)

    def lend():
        return pltpu.make_async_remote_copy(
            qbuf.at[tiles(0)], qbuf.at[tiles(1)], send, q_recv.at[1],
            device_id=at(mate, hub), device_id_type=MESH)

    def result_copy(where, place, side):
        return pltpu.make_async_remote_copy(
            done.at[place * panels + side], got.at[place], r_send, r_recv,
            device_id=at(where, side), device_id_type=MESH)

    def keys_landed(source):
        pltpu.make_async_copy(pair(source), pair(source), k_recv.at[source // INNER]).wait()

    def late_landed(side):
        pltpu.make_async_copy(k_ref, kbuf.at[last * panels + side], k_recv.at[outer + hub - side]).wait()

    def queries_landed(half):
        pltpu.make_async_copy(qbuf.at[tiles(half)], qbuf.at[tiles(half)], q_recv.at[half]).wait()

    def score(source, sides, first, tiles):
        row_base = (source // COLBLK).astype(jnp.float32) * (rows / total_rows)
        left = (source % COLBLK) * BCOLS
        sources = [(row_base, (left + side * cols).astype(jnp.float32) * (1.0 / total_cols)) for side in sides]
        block = kbuf[pl.ds(source * panels + sides[0], len(sides))].reshape(len(sides) * keys, kbuf.shape[-1])
        raw = jnp.dot(block, turned[:, first * queries : (first + tiles) * queries],
                      preferred_element_type=jnp.float32)
        for i in range(tiles):
            absorb(raw[:, i * queries : (i + 1) * queries], sources, rows, cols,
                   total_rows, total_cols, rates, state, tile(first + i))

    def turn_queries(place, count):
        rows_in = pl.ds(place * queries, count * queries)
        turned[:, place * queries : (place + count) * queries] = qbuf[rows_in].T

    def clear():
        state[:, 0] = jnp.full_like(state[:, 0], NEG)
        state[:, 1:] = jnp.zeros_like(state[:, 1:])

    def partial(place):
        return settle(cols, rates, state, tile(place))

    greeted = line + jnp.where(spot != 0, 1, 0) + jnp.where(chip == last, panels, 0)

    @pl.when(core == hub)
    def _():
        own_k = pltpu.make_async_copy(k_ref, kbuf.at[me], k_recv.at[line])
        own_q = pltpu.make_async_copy(q_ref, qbuf.at[tile(hub)], q_recv.at[0])

        def greet(where):
            for side in reversed(range(panels)):
                pl.semaphore_signal(barrier, inc=1, device_id=at(where, side), device_id_type=MESH)

        def answer(where):
            pl.semaphore_signal(ready.at[line], inc=1, device_id=at(where, hub), device_id_type=MESH)

        @pl.when(spot == 0)
        def _():
            greet(mate)

        for side in range(hub):
            pl.semaphore_signal(barrier, inc=1, device_id=at(chip, side), device_id_type=MESH)

        each(line + 1, outer, lambda i: greet(i * INNER + spot))

        @pl.when(chip == 0)
        def _():
            greet(last)

        @pl.when(chip != 0)
        def _():
            pl.semaphore_wait(barrier, greeted)

        each(0, line, lambda i: answer(i * INNER + spot))
        below(lambda copy: copy.start())

        @pl.when(spot != 0)
        def _():
            answer(mate)
            query_copy(mate, panels + hub).start()

        own_k.start()
        own_q.start()
        clear()
        queries_landed(0)

        @pl.when(spot == 0)
        def _():
            pl.semaphore_wait(ready.at[line], 1)
            lend().start()

        turn_queries(0, panels)
        keys_landed(chip)

        def send_up(i):
            pl.semaphore_wait(ready.at[i], 1)
            lift(i * INNER + spot).start()

        def in_turn(turn):
            return jnp.where(turn <= line, line - turn, turn) * INNER + spot

        def arrive(turn):
            source = in_turn(turn)

            @pl.when(source != chip)
            def _():
                keys_landed(source)

            return source

        def take(turn):
            score(arrive(turn), range(panels), 0, 2 * panels)

        early = jnp.where(line == 0, 2, 1)
        turns = jnp.where(chip == 1, outer - 2, outer - 1)
        each(line + 1, outer - 1, send_up)
        each(0, early, lambda turn: score(arrive(turn), range(panels), 0, panels))

        @pl.when(line != outer - 1)
        def _():
            send_up(outer - 1)

        queries_landed(1)
        turn_queries(panels, panels)
        each(0, early, lambda turn: score(in_turn(turn), range(panels), panels, panels))

        def side_at(turn):
            return jnp.where(chip == 1, turn, hub - turn)

        def return_one(side):
            done[panels + side] = partial(panels + side)
            result_copy(mate, 1, side).start()

        def return_pair():
            for turn in range(panels):
                return_one(side_at(turn))

        def return_rest():
            for side in range(hub):
                done[side] = partial(side)
                result_copy(chip, 0, side).start()

        each(early, turns, take)
        final = in_turn(turns)
        keys_landed(final)
        score(final, range(panels), panels, panels)

        @pl.when(chip != 0)
        def _():
            return_pair()

        score(final, range(panels), 0, panels)

        @pl.when(chip == 0)
        def _():
            late_landed(hub)
            score(jnp.int32(last), [hub], 0, panels)
            return_rest()
            score(jnp.int32(last), [hub], panels, panels)
            return_pair()
            late_landed(0)
            score(jnp.int32(last), [0], hub, 1)

        @pl.when(chip == 1)
        def _():
            pltpu.make_async_copy(k_ref, kbuf.at[last * panels], k_recv.at[outer - 1]).wait()
            score(jnp.int32(last), [0], 0, panels)

        @pl.when(chip != 0)
        def _():
            return_rest()

        own = partial(hub)

        all_sent(line - lowest + jnp.where(chip == last, 1, 0) + panels * (outer - 1 - line)
                 + query_slots * jnp.where(spot == 0, panels, 1))
        sent = pl.ds(0, hub + panels)
        pltpu.make_async_copy(done.at[sent], done.at[sent], r_send).wait()
        pltpu.make_async_copy(done.at[0], got.at[1], r_recv).wait()
        merged_ref[...] = merge(own, got[1])

    @pl.when(core != hub)
    def _():
        @pl.when(chip == 0)
        def _():
            for side in range(panels):
                pl.semaphore_signal(barrier, inc=1, device_id=at(last, side), device_id_type=MESH)

        pl.semaphore_wait(barrier, greeted + 1)
        below(lambda copy: copy.start())

        @pl.when(spot != 0)
        def _():
            query_copy(mate, panels + core).start()

        query_copy(chip, core).start()
        key_copy(chip).start()

        @pl.when(chip == 0)
        def _():
            own_q = pltpu.make_async_copy(q_ref, qbuf.at[tile(0)], q_recv.at[0])
            own_q.start()
            clear()
            own_q.wait()
            turn_queries(0, 1)
            late_landed(0)
            score(jnp.int32(last), [0], 0, 1)

        all_sent(line + jnp.where(chip == last, 2, 0) + 1 + query_slots * jnp.where(spot == 0, 1, 2))
        pltpu.make_async_copy(got, got, r_recv).wait()
        both = merge(got[0], got[1])

        @pl.when(chip == 0)
        def _():
            merged_ref[...] = merge(partial(0), both)

        @pl.when(chip != 0)
        def _():
            merged_ref[...] = both


def finish(merged_ref, matched_ref, energy_ref):
    top, total = merged_ref[:LEVELS], merged_ref[LEVELS : 2 * LEVELS]
    energy_ref[...] = top + jnp.log(total)
    matched_ref[:, 0, :] = merged_ref[2 * LEVELS : 3 * LEVELS] / total
    matched_ref[:, 1, :] = merged_ref[3 * LEVELS :] / total


def body(blk, panels, first_frame, second_frame):
    queries, channels = first_frame.shape
    _, rows, cols, _ = second_frame.shape
    keys = second_frame.reshape(rows * cols, channels)
    outer = blk // INNER
    dma = pltpu.SemaphoreType.DMA
    merged = pl.pallas_call(
        functools.partial(kernel, (blk, panels, rows, cols)),
        out_shape=pltpu.VMEM((4 * LEVELS, queries), jnp.float32),
        in_specs=[pl.BlockSpec(memory_space=pl.ANY)] * 2,
        out_specs=pl.BlockSpec(memory_space=pltpu.VMEM),
        scratch_shapes=[
            pltpu.VMEM((2 * panels * queries, channels), jnp.bfloat16),
            pltpu.VMEM((channels, 2 * panels * queries), jnp.bfloat16),
            pltpu.VMEM((blk * panels, rows * cols, channels), jnp.bfloat16),
            pltpu.VMEM((LEVELS, 4, cols, 2 * panels * queries), jnp.float32),
            pltpu.VMEM((2 * panels, 4 * LEVELS, queries), jnp.float32),
            pltpu.VMEM((2, 4 * LEVELS, queries), jnp.float32),
            pltpu.SemaphoreType.REGULAR((outer,)),
            dma, dma((outer + panels,)), dma((2,)), dma, dma,
        ],
        compiler_params=pltpu.CompilerParams(collective_id=0, has_side_effects=True),
        name="corr",
    )(first_frame, keys)
    return pl.pallas_call(
        finish,
        out_shape=(jax.ShapeDtypeStruct((LEVELS, 2, queries), jnp.float32),
                   jax.ShapeDtypeStruct((LEVELS, queries), jnp.float32)),
        in_specs=[pl.BlockSpec(memory_space=pltpu.VMEM)],
        out_specs=(pl.BlockSpec(memory_space=pltpu.VMEM), pl.BlockSpec(memory_space=pltpu.VMEM)),
        name="finish",
    )(pltpu.with_memory_space_constraint(merged, pltpu.VMEM))


def solution(mesh):
    placed = (P(("pairs", "blk", "panel"), None), P(("pairs", "blk"), None, "panel", None))
    return jax.shard_map(
        functools.partial(body, mesh.shape["blk"], mesh.shape["panel"]),
        mesh=mesh,
        in_specs=placed,
        out_specs=(P(None, None, ("pairs", "blk", "panel")), P(None, ("pairs", "blk", "panel"))),
        check_vma=False,
    )
```

```python
import functools
import math

import jax
import jax.numpy as jnp
from jax import lax
from jax.experimental import pallas as pl
from jax.experimental.pallas import tpu as pltpu
from jax.sharding import PartitionSpec as P

LEVELS = 4
COLBLK = 8
BCOLS = 16
INNER = 2
NEG = -1e30
MESH = pl.DeviceIdType.MESH


def absorb(raw, sources, rows, cols, total_rows, total_cols, rates, state, lane):
    n = len(sources)
    q = raw.shape[-1]
    col = lax.broadcasted_iota(jnp.int32, (cols, q), 0)
    values = raw.reshape(n, rows, cols, q)
    for level in range(LEVELS):
        step = 2**level
        if level:
            pairs = values.reshape(n, rows // step, 2, cols, q)
            values = pairs[:, :, 0] + pairs[:, :, 1]
            values = values + pltpu.roll(values, step // 2, 2)
        height = rows // step
        old = state[level, 0, :, lane]
        top = jnp.maximum(old, jnp.max(values, axis=(0, 1)))
        weights = jnp.exp2((values - top) * rates[level])
        decay = jnp.exp2((old - top) * rates[level])
        col_in = ((col >> level).astype(jnp.float32) + 0.5) * (step / total_cols)
        total = state[level, 1, :, lane] * decay
        row_sum = state[level, 2, :, lane] * decay
        col_sum = state[level, 3, :, lane] * decay
        for s, (row_base, col_base) in enumerate(sources):
            part = weights[s, 0]
            part_row = weights[s, 0] * (0.5 * step / total_rows)
            for i in range(1, height):
                part = part + weights[s, i]
                part_row = part_row + weights[s, i] * ((i + 0.5) * step / total_rows)
            total = total + part
            row_sum = row_sum + (part_row + part * row_base)
            col_sum = col_sum + part * (col_in + col_base)
        state[level, 0, :, lane] = top
        state[level, 1, :, lane] = total
        state[level, 2, :, lane] = row_sum
        state[level, 3, :, lane] = col_sum


def settle(cols, rates, state, lane):
    tops, totals, row_sums, col_sums = [], [], [], []
    for level in range(LEVELS):
        step = 2**level
        top = state[level, 0, :, lane]
        col = lax.broadcasted_iota(jnp.int32, top.shape, 0)
        valid = (col & (step - 1)) == step - 1
        best = jnp.max(jnp.where(valid, top, NEG), axis=0, keepdims=True)
        scale = jnp.exp2((top - best) * rates[level])
        for rows_out, i in ((totals, 1), (row_sums, 2), (col_sums, 3)):
            term = jnp.where(valid, state[level, i, :, lane] * scale, 0.0)
            rows_out.append(jnp.sum(term, axis=0, keepdims=True))
        tops.append(best * (rates[level] * math.log(2.0)))
    return jnp.concatenate(tops + totals + row_sums + col_sums, axis=0)


def merge(one, two):
    top = jnp.maximum(one[:LEVELS], two[:LEVELS])
    one_scale, two_scale = jnp.exp(one[:LEVELS] - top), jnp.exp(two[:LEVELS] - top)
    sums = [one[LEVELS * i : LEVELS * (i + 1)] * one_scale + two[LEVELS * i : LEVELS * (i + 1)] * two_scale
            for i in (1, 2, 3)]
    return jnp.concatenate([top] + sums, axis=0)


def kernel(dims, q_ref, k_ref, merged_ref, qbuf, turned, kbuf, state, done, got, ready,
           send, k_recv, q_recv, r_send, r_recv):
    blk, panels, rows, cols = dims
    outer = blk // INNER
    queries = q_ref.shape[0]
    keys = rows * cols
    query_slots = queries // keys
    total_rows, total_cols = rows * blk // COLBLK, BCOLS * COLBLK
    chip, core = lax.axis_index("blk"), lax.axis_index("panel")
    me = chip * panels + core
    hub = panels - 1
    line, spot = chip // INNER, chip % INNER
    mate = line * INNER + (INNER - 1 - spot)
    last = blk - 1
    lowest = jnp.where((chip == last) & (core == hub), 1, 0)
    whole_line = (chip == last) & (core != hub)
    first_part = lax.axis_index("pairs") == 0
    barrier = pltpu.get_barrier_semaphore()
    rates = [3.0 / math.sqrt(k_ref.shape[-1]) / math.log(2.0) / 2**level for level in range(LEVELS)]

    def at(where, side):
        return {"blk": where, "panel": side}

    def each(low, high, step):
        lax.fori_loop(low, high, lambda i, _: (step(i), 0)[1], 0)

    def tile(i):
        return pl.ds(pl.multiple_of(i * queries, queries), queries)

    def tiles(half):
        return pl.ds(half * panels * queries, panels * queries)

    def key_copy(where, side=hub):
        apart = (chip == last) & (where == 0)
        single = (chip == last - INNER) & (core != hub) & (where == 1)
        return pltpu.make_async_remote_copy(
            k_ref, kbuf.at[me], send,
            k_recv.at[jnp.where(single, outer, jnp.where(apart, outer + hub - core, line))],
            device_id=at(where, side), device_id_type=MESH)

    def below(act):
        @pl.when(whole_line)
        def _():
            act(key_copy(0, 0))

            @pl.when(first_part)
            def _():
                act(key_copy(0))

            act(key_copy(INNER + spot))

            @pl.when(jnp.logical_not(first_part))
            def _():
                act(key_copy(0))

            act(key_copy(spot))
            each(2, line, lambda i: act(key_copy(i * INNER + spot)))

        @pl.when((chip == last) & (core == hub))
        def _():
            act(key_copy(0))
            each(2, line, lambda i: act(key_copy(i * INNER + spot)))
            act(key_copy(INNER + spot))

        @pl.when(chip != last)
        def _():
            each(0, line, lambda i: act(key_copy(i * INNER + spot)))

    def all_sent(slots):
        for count in range(1, 2 * outer + 5):
            @pl.when(slots == count)
            def _():
                pltpu.make_async_copy(kbuf.at[:count], kbuf.at[:count], send).wait()

    def query_copy(where, place):
        return pltpu.make_async_remote_copy(
            q_ref, qbuf.at[tile(place)], send, q_recv.at[place // panels],
            device_id=at(where, hub), device_id_type=MESH)

    def pair(chip):
        return kbuf.at[pl.ds(chip * panels, panels)]

    def lift(where):
        return pltpu.make_async_remote_copy(
            pair(chip), pair(chip), send, k_recv.at[line],
            device_id=at(where, hub), device_id_type=MESH)

    def lend():
        return pltpu.make_async_remote_copy(
            qbuf.at[tiles(0)], qbuf.at[tiles(1)], send, q_recv.at[1],
            device_id=at(mate, hub), device_id_type=MESH)

    def result_copy(where, place, side):
        return pltpu.make_async_remote_copy(
            done.at[place * panels + side], got.at[place], r_send, r_recv,
            device_id=at(where, side), device_id_type=MESH)

    def keys_landed(source):
        pltpu.make_async_copy(pair(source), pair(source), k_recv.at[source // INNER]).wait()

    def late_landed(side):
        pltpu.make_async_copy(k_ref, kbuf.at[last * panels + side], k_recv.at[outer + hub - side]).wait()

    def queries_landed(half):
        pltpu.make_async_copy(qbuf.at[tiles(half)], qbuf.at[tiles(half)], q_recv.at[half]).wait()

    def score(source, sides, first, tiles):
        row_base = (source // COLBLK).astype(jnp.float32) * (rows / total_rows)
        left = (source % COLBLK) * BCOLS
        sources = [(row_base, (left + side * cols).astype(jnp.float32) * (1.0 / total_cols)) for side in sides]
        block = kbuf[pl.ds(source * panels + sides[0], len(sides))].reshape(len(sides) * keys, kbuf.shape[-1])
        raw = jnp.dot(block, turned[:, first * queries : (first + tiles) * queries],
                      preferred_element_type=jnp.float32)
        for i in range(tiles):
            absorb(raw[:, i * queries : (i + 1) * queries], sources, rows, cols,
                   total_rows, total_cols, rates, state, tile(first + i))

    def turn_queries(place, count):
        rows_in = pl.ds(place * queries, count * queries)
        turned[:, place * queries : (place + count) * queries] = qbuf[rows_in].T

    def clear():
        state[:, 0] = jnp.full_like(state[:, 0], NEG)
        state[:, 1:] = jnp.zeros_like(state[:, 1:])

    def partial(place):
        return settle(cols, rates, state, tile(place))

    greeted = line + jnp.where(spot != 0, 1, 0) + jnp.where(chip == last, panels, 0)

    @pl.when(core == hub)
    def _():
        own_k = pltpu.make_async_copy(k_ref, kbuf.at[me], k_recv.at[line])
        own_q = pltpu.make_async_copy(q_ref, qbuf.at[tile(hub)], q_recv.at[0])

        def greet(where):
            for side in reversed(range(panels)):
                pl.semaphore_signal(barrier, inc=1, device_id=at(where, side), device_id_type=MESH)

        def answer(where):
            pl.semaphore_signal(ready.at[line], inc=1, device_id=at(where, hub), device_id_type=MESH)

        @pl.when(spot == 0)
        def _():
            greet(mate)

        for side in range(hub):
            pl.semaphore_signal(barrier, inc=1, device_id=at(chip, side), device_id_type=MESH)

        each(line + 1, outer, lambda i: greet(i * INNER + spot))

        @pl.when(chip == 0)
        def _():
            greet(last)

        @pl.when(chip != 0)
        def _():
            pl.semaphore_wait(barrier, greeted)

        each(0, line, lambda i: answer(i * INNER + spot))
        below(lambda copy: copy.start())

        @pl.when(spot != 0)
        def _():
            answer(mate)
            query_copy(mate, panels + hub).start()

        own_k.start()
        own_q.start()
        clear()
        queries_landed(0)

        @pl.when(spot == 0)
        def _():
            pl.semaphore_wait(ready.at[line], 1)
            lend().start()

        turn_queries(0, panels)
        keys_landed(chip)

        def send_up(i):
            pl.semaphore_wait(ready.at[i], 1)
            lift(i * INNER + spot).start()

        def in_turn(turn):
            return jnp.where(turn <= line, line - turn, turn) * INNER + spot

        def arrive(turn):
            source = in_turn(turn)

            @pl.when(source != chip)
            def _():
                keys_landed(source)

            return source

        def take(turn):
            score(arrive(turn), range(panels), 0, 2 * panels)

        early = jnp.where(line == 0, 2, 1)
        turns = jnp.where(chip == 1, outer - 2, outer - 1)
        each(line + 1, outer - 1, send_up)
        each(0, early, lambda turn: score(arrive(turn), range(panels), 0, panels))

        @pl.when(line != outer - 1)
        def _():
            send_up(outer - 1)

        queries_landed(1)
        turn_queries(panels, panels)
        each(0, early, lambda turn: score(in_turn(turn), range(panels), panels, panels))

        def side_at(turn):
            return jnp.where(chip == 1, turn, hub - turn)

        def return_one(side):
            done[panels + side] = partial(panels + side)
            result_copy(mate, 1, side).start()

        def return_pair():
            for turn in range(panels):
                return_one(side_at(turn))

        def return_rest():
            for side in range(hub):
                done[side] = partial(side)
                result_copy(chip, 0, side).start()

        each(early, turns, take)
        final = in_turn(turns)
        @pl.when(chip == 0)
        def _():
            keys_landed(final)
            score(final, range(panels), 0, panels)
            late_landed(hub)
            score(jnp.int32(last), [hub], 0, panels)
            return_rest()
            score(final, range(panels), panels, panels)
            score(jnp.int32(last), [hub], panels, panels)
            return_pair()
            late_landed(0)
            score(jnp.int32(last), [0], hub, 1)

        @pl.when(chip == 1)
        def _():
            pltpu.make_async_copy(k_ref, kbuf.at[final * panels + hub], k_recv.at[outer - 2]).wait()
            score(final, [hub], 0, 2 * panels)
            pltpu.make_async_copy(k_ref, kbuf.at[final * panels], k_recv.at[outer]).wait()
            for side in range(panels):
                score(final, [0], panels + side, 1)
                return_one(side)
            score(final, [0], 0, panels)
            pltpu.make_async_copy(k_ref, kbuf.at[last * panels], k_recv.at[outer - 1]).wait()
            score(jnp.int32(last), [0], 0, panels)

        @pl.when(chip > 1)
        def _():
            keys_landed(final)
            score(final, range(panels), panels, panels)
            return_pair()
            score(final, range(panels), 0, panels)

        @pl.when(chip != 0)
        def _():
            return_rest()

        own = partial(hub)

        all_sent(line - lowest + jnp.where(chip == last, 1, 0) + panels * (outer - 1 - line)
                 + query_slots * jnp.where(spot == 0, panels, 1))
        sent = pl.ds(0, hub + panels)
        pltpu.make_async_copy(done.at[sent], done.at[sent], r_send).wait()
        pltpu.make_async_copy(done.at[0], got.at[1], r_recv).wait()
        merged_ref[...] = merge(own, got[1])

    @pl.when(core != hub)
    def _():
        @pl.when(chip == 0)
        def _():
            for side in range(panels):
                pl.semaphore_signal(barrier, inc=1, device_id=at(last, side), device_id_type=MESH)

        pl.semaphore_wait(barrier, greeted + 1)
        below(lambda copy: copy.start())

        @pl.when(spot != 0)
        def _():
            query_copy(mate, panels + core).start()

        query_copy(chip, core).start()
        key_copy(chip).start()

        @pl.when(chip == 0)
        def _():
            own_q = pltpu.make_async_copy(q_ref, qbuf.at[tile(0)], q_recv.at[0])
            own_q.start()
            clear()
            own_q.wait()
            turn_queries(0, 1)
            late_landed(0)
            score(jnp.int32(last), [0], 0, 1)

        all_sent(line + jnp.where(chip == last, 2, 0) + 1 + query_slots * jnp.where(spot == 0, 1, 2))
        pltpu.make_async_copy(got, got, r_recv).wait()
        both = merge(got[0], got[1])

        @pl.when(chip == 0)
        def _():
            merged_ref[...] = merge(partial(0), both)

        @pl.when(chip != 0)
        def _():
            merged_ref[...] = both


def finish(merged_ref, matched_ref, energy_ref):
    top, total = merged_ref[:LEVELS], merged_ref[LEVELS : 2 * LEVELS]
    energy_ref[...] = top + jnp.log(total)
    matched_ref[:, 0, :] = merged_ref[2 * LEVELS : 3 * LEVELS] / total
    matched_ref[:, 1, :] = merged_ref[3 * LEVELS :] / total


def body(blk, panels, first_frame, second_frame):
    queries, channels = first_frame.shape
    _, rows, cols, _ = second_frame.shape
    keys = second_frame.reshape(rows * cols, channels)
    outer = blk // INNER
    dma = pltpu.SemaphoreType.DMA
    merged = pl.pallas_call(
        functools.partial(kernel, (blk, panels, rows, cols)),
        out_shape=pltpu.VMEM((4 * LEVELS, queries), jnp.float32),
        in_specs=[pl.BlockSpec(memory_space=pl.ANY)] * 2,
        out_specs=pl.BlockSpec(memory_space=pltpu.VMEM),
        scratch_shapes=[
            pltpu.VMEM((2 * panels * queries, channels), jnp.bfloat16),
            pltpu.VMEM((channels, 2 * panels * queries), jnp.bfloat16),
            pltpu.VMEM((blk * panels, rows * cols, channels), jnp.bfloat16),
            pltpu.VMEM((LEVELS, 4, cols, 2 * panels * queries), jnp.float32),
            pltpu.VMEM((2 * panels, 4 * LEVELS, queries), jnp.float32),
            pltpu.VMEM((2, 4 * LEVELS, queries), jnp.float32),
            pltpu.SemaphoreType.REGULAR((outer,)),
            dma, dma((outer + panels,)), dma((2,)), dma, dma,
        ],
        compiler_params=pltpu.CompilerParams(collective_id=0, has_side_effects=True),
        name="corr",
    )(first_frame, keys)
    return pl.pallas_call(
        finish,
        out_shape=(jax.ShapeDtypeStruct((LEVELS, 2, queries), jnp.float32),
                   jax.ShapeDtypeStruct((LEVELS, queries), jnp.float32)),
        in_specs=[pl.BlockSpec(memory_space=pltpu.VMEM)],
        out_specs=(pl.BlockSpec(memory_space=pltpu.VMEM), pl.BlockSpec(memory_space=pltpu.VMEM)),
        name="finish",
    )(pltpu.with_memory_space_constraint(merged, pltpu.VMEM))


def solution(mesh):
    placed = (P(("pairs", "blk", "panel"), None), P(("pairs", "blk"), None, "panel", None))
    return jax.shard_map(
        functools.partial(body, mesh.shape["blk"], mesh.shape["panel"]),
        mesh=mesh,
        in_specs=placed,
        out_specs=(P(None, None, ("pairs", "blk", "panel")), P(None, ("pairs", "blk", "panel"))),
        check_vma=False,
    )
```

```python
import functools
import math

import jax
import jax.numpy as jnp
from jax import lax
from jax.experimental import pallas as pl
from jax.experimental.pallas import tpu as pltpu
from jax.sharding import PartitionSpec as P

LEVELS = 4
COLBLK = 8
BCOLS = 16
INNER = 2
NEG = -1e30
MESH = pl.DeviceIdType.MESH


def absorb(raw, sources, rows, cols, total_rows, total_cols, rates, state, lane):
    n = len(sources)
    q = raw.shape[-1]
    col = lax.broadcasted_iota(jnp.int32, (cols, q), 0)
    values = raw.reshape(n, rows, cols, q)
    for level in range(LEVELS):
        step = 2**level
        if level:
            pairs = values.reshape(n, rows // step, 2, cols, q)
            values = pairs[:, :, 0] + pairs[:, :, 1]
            values = values + pltpu.roll(values, step // 2, 2)
        height = rows // step
        old = state[level, 0, :, lane]
        top = jnp.maximum(old, jnp.max(values, axis=(0, 1)))
        weights = jnp.exp2((values - top) * rates[level])
        decay = jnp.exp2((old - top) * rates[level])
        col_in = ((col >> level).astype(jnp.float32) + 0.5) * (step / total_cols)
        total = state[level, 1, :, lane] * decay
        row_sum = state[level, 2, :, lane] * decay
        col_sum = state[level, 3, :, lane] * decay
        for s, (row_base, col_base) in enumerate(sources):
            part = weights[s, 0]
            part_row = weights[s, 0] * (0.5 * step / total_rows)
            for i in range(1, height):
                part = part + weights[s, i]
                part_row = part_row + weights[s, i] * ((i + 0.5) * step / total_rows)
            total = total + part
            row_sum = row_sum + (part_row + part * row_base)
            col_sum = col_sum + part * (col_in + col_base)
        state[level, 0, :, lane] = top
        state[level, 1, :, lane] = total
        state[level, 2, :, lane] = row_sum
        state[level, 3, :, lane] = col_sum


def settle(cols, rates, state, lane):
    tops, totals, row_sums, col_sums = [], [], [], []
    for level in range(LEVELS):
        step = 2**level
        top = state[level, 0, :, lane]
        col = lax.broadcasted_iota(jnp.int32, top.shape, 0)
        valid = (col & (step - 1)) == step - 1
        best = jnp.max(jnp.where(valid, top, NEG), axis=0, keepdims=True)
        scale = jnp.exp2((top - best) * rates[level])
        for rows_out, i in ((totals, 1), (row_sums, 2), (col_sums, 3)):
            term = jnp.where(valid, state[level, i, :, lane] * scale, 0.0)
            rows_out.append(jnp.sum(term, axis=0, keepdims=True))
        tops.append(best * (rates[level] * math.log(2.0)))
    return jnp.concatenate(tops + totals + row_sums + col_sums, axis=0)


def merge(one, two):
    top = jnp.maximum(one[:LEVELS], two[:LEVELS])
    one_scale, two_scale = jnp.exp(one[:LEVELS] - top), jnp.exp(two[:LEVELS] - top)
    sums = [one[LEVELS * i : LEVELS * (i + 1)] * one_scale + two[LEVELS * i : LEVELS * (i + 1)] * two_scale
            for i in (1, 2, 3)]
    return jnp.concatenate([top] + sums, axis=0)


def kernel(dims, q_ref, k_ref, merged_ref, qbuf, turned, kbuf, state, done, got, ready,
           send, k_recv, q_recv, r_send, r_recv):
    blk, panels, rows, cols = dims
    outer = blk // INNER
    queries = q_ref.shape[0]
    keys = rows * cols
    query_slots = queries // keys
    total_rows, total_cols = rows * blk // COLBLK, BCOLS * COLBLK
    chip, core = lax.axis_index("blk"), lax.axis_index("panel")
    me = chip * panels + core
    hub = panels - 1
    line, spot = chip // INNER, chip % INNER
    mate = line * INNER + (INNER - 1 - spot)
    last = blk - 1
    lowest = jnp.where((chip == last) & (core == hub), 1, 0)
    whole_line = (chip == last) & (core != hub)
    first_part = lax.axis_index("pairs") == 0
    barrier = pltpu.get_barrier_semaphore()
    rates = [3.0 / math.sqrt(k_ref.shape[-1]) / math.log(2.0) / 2**level for level in range(LEVELS)]

    def at(where, side):
        return {"blk": where, "panel": side}

    def each(low, high, step):
        lax.fori_loop(low, high, lambda i, _: (step(i), 0)[1], 0)

    def tile(i):
        return pl.ds(pl.multiple_of(i * queries, queries), queries)

    def tiles(half):
        return pl.ds(half * panels * queries, panels * queries)

    def key_copy(where, side=hub):
        apart = (chip == last) & (where == 0)
        single = (chip == last - INNER) & (core != hub) & (where == 1)
        return pltpu.make_async_remote_copy(
            k_ref, kbuf.at[me], send,
            k_recv.at[jnp.where(single, outer, jnp.where(apart, outer + hub - core, line))],
            device_id=at(where, side), device_id_type=MESH)

    def below(act):
        @pl.when(whole_line)
        def _():
            act(key_copy(0, 0))

            @pl.when(first_part)
            def _():
                act(key_copy(0))

            act(key_copy(INNER + spot))

            @pl.when(jnp.logical_not(first_part))
            def _():
                act(key_copy(0))

            act(key_copy(spot))
            each(2, line, lambda i: act(key_copy(i * INNER + spot)))

        @pl.when((chip == last) & (core == hub))
        def _():
            act(key_copy(0))
            each(2, line, lambda i: act(key_copy(i * INNER + spot)))
            act(key_copy(INNER + spot))

        @pl.when(chip != last)
        def _():
            each(0, line, lambda i: act(key_copy(i * INNER + spot)))

    def all_sent(slots):
        for count in range(1, 2 * outer + 5):
            @pl.when(slots == count)
            def _():
                pltpu.make_async_copy(kbuf.at[:count], kbuf.at[:count], send).wait()

    def query_copy(where, place):
        return pltpu.make_async_remote_copy(
            q_ref, qbuf.at[tile(place)], send, q_recv.at[place // panels],
            device_id=at(where, hub), device_id_type=MESH)

    def pair(chip):
        return kbuf.at[pl.ds(chip * panels, panels)]

    def lift(where):
        return pltpu.make_async_remote_copy(
            pair(chip), pair(chip), send, k_recv.at[line],
            device_id=at(where, hub), device_id_type=MESH)

    def lend():
        return pltpu.make_async_remote_copy(
            qbuf.at[tiles(0)], qbuf.at[tiles(1)], send, q_recv.at[1],
            device_id=at(mate, hub), device_id_type=MESH)

    def result_copy(where, place, side):
        return pltpu.make_async_remote_copy(
            done.at[place * panels + side], got.at[place], r_send, r_recv,
            device_id=at(where, side), device_id_type=MESH)

    def keys_landed(source):
        pltpu.make_async_copy(pair(source), pair(source), k_recv.at[source // INNER]).wait()

    def late_landed(side):
        pltpu.make_async_copy(k_ref, kbuf.at[last * panels + side], k_recv.at[outer + hub - side]).wait()

    def queries_landed(half):
        pltpu.make_async_copy(qbuf.at[tiles(half)], qbuf.at[tiles(half)], q_recv.at[half]).wait()

    def score(source, sides, first, tiles):
        row_base = (source // COLBLK).astype(jnp.float32) * (rows / total_rows)
        left = (source % COLBLK) * BCOLS
        sources = [(row_base, (left + side * cols).astype(jnp.float32) * (1.0 / total_cols)) for side in sides]
        block = kbuf[pl.ds(source * panels + sides[0], len(sides))].reshape(len(sides) * keys, kbuf.shape[-1])
        raw = jnp.dot(block, turned[:, first * queries : (first + tiles) * queries],
                      preferred_element_type=jnp.float32)
        for i in range(tiles):
            absorb(raw[:, i * queries : (i + 1) * queries], sources, rows, cols,
                   total_rows, total_cols, rates, state, tile(first + i))

    def turn_queries(place, count):
        rows_in = pl.ds(place * queries, count * queries)
        turned[:, place * queries : (place + count) * queries] = qbuf[rows_in].T

    def clear():
        state[:, 0] = jnp.full_like(state[:, 0], NEG)
        state[:, 1:] = jnp.zeros_like(state[:, 1:])

    def partial(place):
        return settle(cols, rates, state, tile(place))

    lends = (spot == 0) | (line > 0)
    met = (spot != 0) & ((line == 0) | (core == hub))
    greeted = line + jnp.where(met, 1, 0) + jnp.where(chip == last, panels, 0)

    @pl.when(core == hub)
    def _():
        own_k = pltpu.make_async_copy(k_ref, kbuf.at[me], k_recv.at[line])
        own_q = pltpu.make_async_copy(q_ref, qbuf.at[tile(hub)], q_recv.at[0])

        def greet(where):
            for side in reversed(range(panels)):
                pl.semaphore_signal(barrier, inc=1, device_id=at(where, side), device_id_type=MESH)

        def answer(where):
            pl.semaphore_signal(ready.at[line], inc=1, device_id=at(where, hub), device_id_type=MESH)

        @pl.when(spot == 0)
        def _():
            pl.semaphore_signal(barrier, inc=1, device_id=at(mate, hub), device_id_type=MESH)

        @pl.when(chip == 0)
        def _():
            for side in range(hub):
                pl.semaphore_signal(barrier, inc=1, device_id=at(mate, side), device_id_type=MESH)

        for side in range(hub):
            pl.semaphore_signal(barrier, inc=1, device_id=at(chip, side), device_id_type=MESH)

        each(line + 1, outer, lambda i: greet(i * INNER + spot))

        @pl.when(chip == 0)
        def _():
            greet(last)

        @pl.when(chip != 0)
        def _():
            pl.semaphore_wait(barrier, greeted)

        each(0, line, lambda i: answer(i * INNER + spot))
        below(lambda copy: copy.start())

        @pl.when(spot != 0)
        def _():
            answer(mate)

        @pl.when(chip == 1)
        def _():
            query_copy(mate, panels + hub).start()

        own_k.start()
        own_q.start()
        clear()
        queries_landed(0)

        @pl.when(spot == 0)
        def _():
            pl.semaphore_wait(ready.at[line], 1)

        @pl.when(lends)
        def _():
            lend().start()

        turn_queries(0, panels)
        keys_landed(chip)

        def send_up(i):
            pl.semaphore_wait(ready.at[i], 1)
            lift(i * INNER + spot).start()

        def in_turn(turn):
            return jnp.where(turn <= line, line - turn, turn) * INNER + spot

        def arrive(turn):
            source = in_turn(turn)

            @pl.when(source != chip)
            def _():
                keys_landed(source)

            return source

        def take(turn):
            score(arrive(turn), range(panels), 0, 2 * panels)

        early = jnp.where(line == 0, 2, 1)
        turns = jnp.where(chip == 1, outer - 2, outer - 1)
        each(line + 1, outer - 1, send_up)
        each(0, early, lambda turn: score(arrive(turn), range(panels), 0, panels))

        @pl.when(line != outer - 1)
        def _():
            send_up(outer - 1)

        queries_landed(1)
        turn_queries(panels, panels)
        each(0, early, lambda turn: score(in_turn(turn), range(panels), panels, panels))

        def side_at(turn):
            return jnp.where(chip == 1, turn, hub - turn)

        def return_one(side):
            done[panels + side] = partial(panels + side)
            result_copy(mate, 1, side).start()

        def return_pair():
            for turn in range(panels):
                return_one(side_at(turn))

        def return_rest():
            for side in range(hub):
                done[side] = partial(side)
                result_copy(chip, 0, side).start()

        each(early, turns, take)
        final = in_turn(turns)
        @pl.when(chip == 0)
        def _():
            keys_landed(final)
            score(final, range(panels), 0, panels)
            late_landed(hub)
            score(jnp.int32(last), [hub], 0, panels)
            return_rest()
            score(final, range(panels), panels, panels)
            score(jnp.int32(last), [hub], panels, panels)
            return_pair()
            late_landed(0)
            score(jnp.int32(last), [0], hub, 1)

        @pl.when(chip == 1)
        def _():
            pltpu.make_async_copy(k_ref, kbuf.at[final * panels + hub], k_recv.at[outer - 2]).wait()
            score(final, [hub], panels, panels)
            pltpu.make_async_copy(k_ref, kbuf.at[final * panels], k_recv.at[outer]).wait()
            for side in range(panels):
                score(final, [0], panels + side, 1)
                return_one(side)
            score(final, range(panels), 0, panels)
            pltpu.make_async_copy(k_ref, kbuf.at[last * panels], k_recv.at[outer - 1]).wait()
            score(jnp.int32(last), [0], 0, panels)

        @pl.when(chip > 1)
        def _():
            keys_landed(final)
            score(final, range(panels), panels, panels)
            return_pair()
            score(final, range(panels), 0, panels)

        @pl.when(chip != 0)
        def _():
            return_rest()

        own = partial(hub)

        all_sent(line - lowest + jnp.where(chip == last, 1, 0) + panels * (outer - 1 - line)
                 + query_slots * jnp.where(lends, panels, 1))
        sent = pl.ds(0, hub + panels)
        pltpu.make_async_copy(done.at[sent], done.at[sent], r_send).wait()
        pltpu.make_async_copy(done.at[0], got.at[1], r_recv).wait()
        merged_ref[...] = merge(own, got[1])

    @pl.when(core != hub)
    def _():
        @pl.when(chip == 0)
        def _():
            for side in range(panels):
                pl.semaphore_signal(barrier, inc=1, device_id=at(last, side), device_id_type=MESH)

        pl.semaphore_wait(barrier, greeted + 1)
        below(lambda copy: copy.start())

        @pl.when(chip == 1)
        def _():
            query_copy(mate, panels + core).start()

        query_copy(chip, core).start()
        key_copy(chip).start()

        @pl.when(chip == 0)
        def _():
            own_q = pltpu.make_async_copy(q_ref, qbuf.at[tile(0)], q_recv.at[0])
            own_q.start()
            clear()
            own_q.wait()
            turn_queries(0, 1)
            late_landed(0)
            score(jnp.int32(last), [0], 0, 1)
            done[0] = partial(0)

        all_sent(line + jnp.where(chip == last, 2, 0) + 1 + query_slots * jnp.where(lends, 1, 2))
        pltpu.make_async_copy(got, got, r_recv).wait()
        both = merge(got[0], got[1])

        @pl.when(chip == 0)
        def _():
            merged_ref[...] = merge(done[0], both)

        @pl.when(chip != 0)
        def _():
            merged_ref[...] = both


def finish(merged_ref, matched_ref, energy_ref):
    top, total = merged_ref[:LEVELS], merged_ref[LEVELS : 2 * LEVELS]
    energy_ref[...] = top + jnp.log(total)
    matched_ref[:, 0, :] = merged_ref[2 * LEVELS : 3 * LEVELS] / total
    matched_ref[:, 1, :] = merged_ref[3 * LEVELS :] / total


def body(blk, panels, first_frame, second_frame):
    queries, channels = first_frame.shape
    _, rows, cols, _ = second_frame.shape
    keys = second_frame.reshape(rows * cols, channels)
    outer = blk // INNER
    dma = pltpu.SemaphoreType.DMA
    merged = pl.pallas_call(
        functools.partial(kernel, (blk, panels, rows, cols)),
        out_shape=pltpu.VMEM((4 * LEVELS, queries), jnp.float32),
        in_specs=[pl.BlockSpec(memory_space=pl.ANY)] * 2,
        out_specs=pl.BlockSpec(memory_space=pltpu.VMEM),
        scratch_shapes=[
            pltpu.VMEM((2 * panels * queries, channels), jnp.bfloat16),
            pltpu.VMEM((channels, 2 * panels * queries), jnp.bfloat16),
            pltpu.VMEM((blk * panels, rows * cols, channels), jnp.bfloat16),
            pltpu.VMEM((LEVELS, 4, cols, 2 * panels * queries), jnp.float32),
            pltpu.VMEM((2 * panels, 4 * LEVELS, queries), jnp.float32),
            pltpu.VMEM((2, 4 * LEVELS, queries), jnp.float32),
            pltpu.SemaphoreType.REGULAR((outer,)),
            dma, dma((outer + panels,)), dma((2,)), dma, dma,
        ],
        compiler_params=pltpu.CompilerParams(collective_id=0, has_side_effects=True),
        name="corr",
    )(first_frame, keys)
    return pl.pallas_call(
        finish,
        out_shape=(jax.ShapeDtypeStruct((LEVELS, 2, queries), jnp.float32),
                   jax.ShapeDtypeStruct((LEVELS, queries), jnp.float32)),
        in_specs=[pl.BlockSpec(memory_space=pltpu.VMEM)],
        out_specs=(pl.BlockSpec(memory_space=pltpu.VMEM), pl.BlockSpec(memory_space=pltpu.VMEM)),
        name="finish",
    )(pltpu.with_memory_space_constraint(merged, pltpu.VMEM))


def solution(mesh):
    placed = (P(("pairs", "blk", "panel"), None), P(("pairs", "blk"), None, "panel", None))
    return jax.shard_map(
        functools.partial(body, mesh.shape["blk"], mesh.shape["panel"]),
        mesh=mesh,
        in_specs=placed,
        out_specs=(P(None, None, ("pairs", "blk", "panel")), P(None, ("pairs", "blk", "panel"))),
        check_vma=False,
    )
```

```python
import functools
import math

import jax
import jax.numpy as jnp
from jax import lax
from jax.experimental import pallas as pl
from jax.experimental.pallas import tpu as pltpu
from jax.sharding import PartitionSpec as P

LEVELS = 4
COLBLK = 8
BCOLS = 16
INNER = 2
NEG = -1e30
MESH = pl.DeviceIdType.MESH


def absorb(raw, sources, rows, cols, total_rows, total_cols, rates, state, lane):
    n = len(sources)
    q = raw.shape[-1]
    col = lax.broadcasted_iota(jnp.int32, (cols, q), 0)
    values = raw.reshape(n, rows, cols, q)
    for level in range(LEVELS):
        step = 2**level
        if level:
            pairs = values.reshape(n, rows // step, 2, cols, q)
            values = pairs[:, :, 0] + pairs[:, :, 1]
            values = values + pltpu.roll(values, step // 2, 2)
        height = rows // step
        old = state[level, 0, :, lane]
        top = jnp.maximum(old, jnp.max(values, axis=(0, 1)))
        weights = jnp.exp2((values - top) * rates[level])
        decay = jnp.exp2((old - top) * rates[level])
        col_in = ((col >> level).astype(jnp.float32) + 0.5) * (step / total_cols)
        total = state[level, 1, :, lane] * decay
        row_sum = state[level, 2, :, lane] * decay
        col_sum = state[level, 3, :, lane] * decay
        for s, (row_base, col_base) in enumerate(sources):
            part = weights[s, height - 1]
            ranked = part if height > 1 else None
            for i in range(height - 2, -1, -1):
                part = part + weights[s, i]
                ranked = ranked + part if i else ranked
            half = 0.5 * part
            part_row = (half if ranked is None else ranked + half) * (step / total_rows)
            total = total + part
            row_sum = row_sum + (part_row + part * row_base)
            col_sum = col_sum + part * (col_in + col_base)
        state[level, 0, :, lane] = top
        state[level, 1, :, lane] = total
        state[level, 2, :, lane] = row_sum
        state[level, 3, :, lane] = col_sum


def settle(cols, rates, state, lane):
    tops, totals, row_sums, col_sums = [], [], [], []
    for level in range(LEVELS):
        step = 2**level
        top = state[level, 0, :, lane]
        col = lax.broadcasted_iota(jnp.int32, top.shape, 0)
        valid = (col & (step - 1)) == step - 1
        best = jnp.max(jnp.where(valid, top, NEG), axis=0, keepdims=True)
        scale = jnp.exp2((top - best) * rates[level])
        for rows_out, i in ((totals, 1), (row_sums, 2), (col_sums, 3)):
            term = jnp.where(valid, state[level, i, :, lane] * scale, 0.0)
            rows_out.append(jnp.sum(term, axis=0, keepdims=True))
        tops.append(best * (rates[level] * math.log(2.0)))
    return jnp.concatenate(tops + totals + row_sums + col_sums, axis=0)


def merge(one, two):
    top = jnp.maximum(one[:LEVELS], two[:LEVELS])
    one_scale, two_scale = jnp.exp(one[:LEVELS] - top), jnp.exp(two[:LEVELS] - top)
    sums = [one[LEVELS * i : LEVELS * (i + 1)] * one_scale + two[LEVELS * i : LEVELS * (i + 1)] * two_scale
            for i in (1, 2, 3)]
    return jnp.concatenate([top] + sums, axis=0)


def kernel(dims, q_ref, k_ref, merged_ref, qbuf, turned, kbuf, state, done, got, ready,
           send, k_recv, q_recv, r_send, r_recv):
    blk, panels, rows, cols = dims
    outer = blk // INNER
    queries = q_ref.shape[0]
    keys = rows * cols
    query_slots = queries // keys
    total_rows, total_cols = rows * blk // COLBLK, BCOLS * COLBLK
    chip, core = lax.axis_index("blk"), lax.axis_index("panel")
    me = chip * panels + core
    hub = panels - 1
    line, spot = chip // INNER, chip % INNER
    mate = line * INNER + (INNER - 1 - spot)
    last = blk - 1
    lowest = jnp.where((chip == last) & (core == hub), 1, 0)
    whole_line = (chip == last) & (core != hub)
    first_part = lax.axis_index("pairs") == 0
    barrier = pltpu.get_barrier_semaphore()
    rates = [3.0 / math.sqrt(k_ref.shape[-1]) / math.log(2.0) / 2**level for level in range(LEVELS)]

    def at(where, side):
        return {"blk": where, "panel": side}

    def each(low, high, step):
        lax.fori_loop(low, high, lambda i, _: (step(i), 0)[1], 0)

    def tile(i):
        return pl.ds(pl.multiple_of(i * queries, queries), queries)

    def tiles(half):
        return pl.ds(half * panels * queries, panels * queries)

    def key_copy(where, side=hub):
        apart = (chip == last) & (where == 0)
        single = (chip == last - INNER) & (core != hub) & (where == 1)
        return pltpu.make_async_remote_copy(
            k_ref, kbuf.at[me], send,
            k_recv.at[jnp.where(single, outer, jnp.where(apart, outer + hub - core, line))],
            device_id=at(where, side), device_id_type=MESH)

    def below(act):
        @pl.when(whole_line)
        def _():
            act(key_copy(0, 0))

            @pl.when(first_part)
            def _():
                act(key_copy(0))

            act(key_copy(INNER + spot))

            @pl.when(jnp.logical_not(first_part))
            def _():
                act(key_copy(0))

            act(key_copy(spot))
            each(2, line, lambda i: act(key_copy(i * INNER + spot)))

        @pl.when((chip == last) & (core == hub))
        def _():
            act(key_copy(0))
            each(2, line, lambda i: act(key_copy(i * INNER + spot)))
            act(key_copy(INNER + spot))

        @pl.when(chip != last)
        def _():
            each(0, line, lambda i: act(key_copy(i * INNER + spot)))

    def all_sent(slots):
        for count in range(1, 2 * outer + 5):
            @pl.when(slots == count)
            def _():
                pltpu.make_async_copy(kbuf.at[:count], kbuf.at[:count], send).wait()

    def query_copy(where, place):
        return pltpu.make_async_remote_copy(
            q_ref, qbuf.at[tile(place)], send, q_recv.at[place // panels],
            device_id=at(where, hub), device_id_type=MESH)

    def pair(chip):
        return kbuf.at[pl.ds(chip * panels, panels)]

    def lift(where):
        return pltpu.make_async_remote_copy(
            pair(chip), pair(chip), send, k_recv.at[line],
            device_id=at(where, hub), device_id_type=MESH)

    def lend():
        return pltpu.make_async_remote_copy(
            qbuf.at[tiles(0)], qbuf.at[tiles(1)], send, q_recv.at[1],
            device_id=at(mate, hub), device_id_type=MESH)

    def result_copy(where, place, side):
        return pltpu.make_async_remote_copy(
            done.at[place * panels + side], got.at[place], r_send, r_recv,
            device_id=at(where, side), device_id_type=MESH)

    def keys_landed(source):
        pltpu.make_async_copy(pair(source), pair(source), k_recv.at[source // INNER]).wait()

    def late_landed(side):
        pltpu.make_async_copy(k_ref, kbuf.at[last * panels + side], k_recv.at[outer + hub - side]).wait()

    def queries_landed(half):
        pltpu.make_async_copy(qbuf.at[tiles(half)], qbuf.at[tiles(half)], q_recv.at[half]).wait()

    def score(source, sides, first, tiles):
        row_base = (source // COLBLK).astype(jnp.float32) * (rows / total_rows)
        left = (source % COLBLK) * BCOLS
        sources = [(row_base, (left + side * cols).astype(jnp.float32) * (1.0 / total_cols)) for side in sides]
        block = kbuf[pl.ds(source * panels + sides[0], len(sides))].reshape(len(sides) * keys, kbuf.shape[-1])
        raw = jnp.dot(block, turned[:, first * queries : (first + tiles) * queries],
                      preferred_element_type=jnp.float32)
        for i in range(tiles):
            absorb(raw[:, i * queries : (i + 1) * queries], sources, rows, cols,
                   total_rows, total_cols, rates, state, tile(first + i))

    def turn_queries(place, count):
        rows_in = pl.ds(place * queries, count * queries)
        turned[:, place * queries : (place + count) * queries] = qbuf[rows_in].T

    def clear():
        state[:, 0] = jnp.full_like(state[:, 0], NEG)
        state[:, 1:] = jnp.zeros_like(state[:, 1:])

    def partial(place):
        return settle(cols, rates, state, tile(place))

    lends = (spot == 0) | (line > 0)
    met = (spot != 0) & ((line == 0) | (core == hub))
    greeted = line + jnp.where(met, 1, 0) + jnp.where(chip == last, panels, 0)

    @pl.when(core == hub)
    def _():
        own_k = pltpu.make_async_copy(k_ref, kbuf.at[me], k_recv.at[line])
        own_q = pltpu.make_async_copy(q_ref, qbuf.at[tile(hub)], q_recv.at[0])

        def greet(where):
            for side in reversed(range(panels)):
                pl.semaphore_signal(barrier, inc=1, device_id=at(where, side), device_id_type=MESH)

        def answer(where):
            pl.semaphore_signal(ready.at[line], inc=1, device_id=at(where, hub), device_id_type=MESH)

        @pl.when(spot == 0)
        def _():
            pl.semaphore_signal(barrier, inc=1, device_id=at(mate, hub), device_id_type=MESH)

        @pl.when(chip == 0)
        def _():
            for side in range(hub):
                pl.semaphore_signal(barrier, inc=1, device_id=at(mate, side), device_id_type=MESH)

        for side in range(hub):
            pl.semaphore_signal(barrier, inc=1, device_id=at(chip, side), device_id_type=MESH)

        each(line + 1, outer, lambda i: greet(i * INNER + spot))

        @pl.when(chip == 0)
        def _():
            greet(last)

        @pl.when(chip != 0)
        def _():
            pl.semaphore_wait(barrier, greeted)

        each(0, line, lambda i: answer(i * INNER + spot))
        below(lambda copy: copy.start())

        @pl.when(spot != 0)
        def _():
            answer(mate)

        @pl.when(chip == 1)
        def _():
            query_copy(mate, panels + hub).start()

        own_k.start()
        own_q.start()
        clear()
        queries_landed(0)

        @pl.when(spot == 0)
        def _():
            pl.semaphore_wait(ready.at[line], 1)

        @pl.when(lends)
        def _():
            lend().start()

        turn_queries(0, panels)
        keys_landed(chip)

        def send_up(i):
            pl.semaphore_wait(ready.at[i], 1)
            lift(i * INNER + spot).start()

        def in_turn(turn):
            return jnp.where(turn <= line, line - turn, turn) * INNER + spot

        def arrive(turn):
            source = in_turn(turn)

            @pl.when(source != chip)
            def _():
                keys_landed(source)

            return source

        def take(turn):
            score(arrive(turn), range(panels), 0, 2 * panels)

        early = jnp.where(line == 0, 2, 1)
        turns = jnp.where(chip == 1, outer - 2, outer - 1)
        each(line + 1, outer - 1, send_up)
        each(0, early, lambda turn: score(arrive(turn), range(panels), 0, panels))

        @pl.when(line != outer - 1)
        def _():
            send_up(outer - 1)

        queries_landed(1)
        turn_queries(panels, panels)
        each(0, early, lambda turn: score(in_turn(turn), range(panels), panels, panels))

        def side_at(turn):
            return jnp.where(chip == 1, turn, hub - turn)

        def return_one(side):
            done[panels + side] = partial(panels + side)
            result_copy(mate, 1, side).start()

        def return_pair():
            for turn in range(panels):
                return_one(side_at(turn))

        def return_rest():
            for side in range(hub):
                done[side] = partial(side)
                result_copy(chip, 0, side).start()

        each(early, turns, take)
        final = in_turn(turns)
        @pl.when(chip == 0)
        def _():
            keys_landed(final)
            score(final, range(panels), 0, panels)
            late_landed(hub)
            score(jnp.int32(last), [hub], 0, panels)
            return_rest()
            score(final, range(panels), panels, panels)
            score(jnp.int32(last), [hub], panels, panels)
            return_pair()
            late_landed(0)
            score(jnp.int32(last), [0], hub, 1)

        @pl.when(chip == 1)
        def _():
            pltpu.make_async_copy(k_ref, kbuf.at[final * panels + hub], k_recv.at[outer - 2]).wait()
            score(final, [hub], panels, panels)
            pltpu.make_async_copy(k_ref, kbuf.at[final * panels], k_recv.at[outer]).wait()
            for side in range(panels):
                score(final, [0], panels + side, 1)
                return_one(side)
            score(final, range(panels), 0, panels)
            pltpu.make_async_copy(k_ref, kbuf.at[last * panels], k_recv.at[outer - 1]).wait()
            score(jnp.int32(last), [0], 0, panels)

        @pl.when(chip > 1)
        def _():
            keys_landed(final)
            score(final, range(panels), panels, panels)
            return_pair()
            score(final, range(panels), 0, panels)

        @pl.when(chip != 0)
        def _():
            return_rest()

        own = partial(hub)

        all_sent(line - lowest + jnp.where(chip == last, 1, 0) + panels * (outer - 1 - line)
                 + query_slots * jnp.where(lends, panels, 1))
        sent = pl.ds(0, hub + panels)
        pltpu.make_async_copy(done.at[sent], done.at[sent], r_send).wait()
        pltpu.make_async_copy(done.at[0], got.at[1], r_recv).wait()
        merged_ref[...] = merge(own, got[1])

    @pl.when(core != hub)
    def _():
        @pl.when(chip == 0)
        def _():
            for side in range(panels):
                pl.semaphore_signal(barrier, inc=1, device_id=at(last, side), device_id_type=MESH)

        pl.semaphore_wait(barrier, greeted + 1)
        below(lambda copy: copy.start())

        @pl.when(chip == 1)
        def _():
            query_copy(mate, panels + core).start()

        query_copy(chip, core).start()
        key_copy(chip).start()

        @pl.when(chip == 0)
        def _():
            own_q = pltpu.make_async_copy(q_ref, qbuf.at[tile(0)], q_recv.at[0])
            own_q.start()
            clear()
            own_q.wait()
            turn_queries(0, 1)
            late_landed(0)
            score(jnp.int32(last), [0], 0, 1)
            done[0] = partial(0)

        all_sent(line + jnp.where(chip == last, 2, 0) + 1 + query_slots * jnp.where(lends, 1, 2))
        pltpu.make_async_copy(got, got, r_recv).wait()
        both = merge(got[0], got[1])

        @pl.when(chip == 0)
        def _():
            merged_ref[...] = merge(done[0], both)

        @pl.when(chip != 0)
        def _():
            merged_ref[...] = both


def finish(merged_ref, matched_ref, energy_ref):
    top, total = merged_ref[:LEVELS], merged_ref[LEVELS : 2 * LEVELS]
    energy_ref[...] = top + jnp.log(total)
    matched_ref[:, 0, :] = merged_ref[2 * LEVELS : 3 * LEVELS] / total
    matched_ref[:, 1, :] = merged_ref[3 * LEVELS :] / total


def body(blk, panels, first_frame, second_frame):
    queries, channels = first_frame.shape
    _, rows, cols, _ = second_frame.shape
    keys = second_frame.reshape(rows * cols, channels)
    outer = blk // INNER
    dma = pltpu.SemaphoreType.DMA
    merged = pl.pallas_call(
        functools.partial(kernel, (blk, panels, rows, cols)),
        out_shape=pltpu.VMEM((4 * LEVELS, queries), jnp.float32),
        in_specs=[pl.BlockSpec(memory_space=pl.ANY)] * 2,
        out_specs=pl.BlockSpec(memory_space=pltpu.VMEM),
        scratch_shapes=[
            pltpu.VMEM((2 * panels * queries, channels), jnp.bfloat16),
            pltpu.VMEM((channels, 2 * panels * queries), jnp.bfloat16),
            pltpu.VMEM((blk * panels, rows * cols, channels), jnp.bfloat16),
            pltpu.VMEM((LEVELS, 4, cols, 2 * panels * queries), jnp.float32),
            pltpu.VMEM((2 * panels, 4 * LEVELS, queries), jnp.float32),
            pltpu.VMEM((2, 4 * LEVELS, queries), jnp.float32),
            pltpu.SemaphoreType.REGULAR((outer,)),
            dma, dma((outer + panels,)), dma((2,)), dma, dma,
        ],
        compiler_params=pltpu.CompilerParams(collective_id=0, has_side_effects=True),
        name="corr",
    )(first_frame, keys)
    return pl.pallas_call(
        finish,
        out_shape=(jax.ShapeDtypeStruct((LEVELS, 2, queries), jnp.float32),
                   jax.ShapeDtypeStruct((LEVELS, queries), jnp.float32)),
        in_specs=[pl.BlockSpec(memory_space=pltpu.VMEM)],
        out_specs=(pl.BlockSpec(memory_space=pltpu.VMEM), pl.BlockSpec(memory_space=pltpu.VMEM)),
        name="finish",
    )(pltpu.with_memory_space_constraint(merged, pltpu.VMEM))


def solution(mesh):
    placed = (P(("pairs", "blk", "panel"), None), P(("pairs", "blk"), None, "panel", None))
    return jax.shard_map(
        functools.partial(body, mesh.shape["blk"], mesh.shape["panel"]),
        mesh=mesh,
        in_specs=placed,
        out_specs=(P(None, None, ("pairs", "blk", "panel")), P(None, ("pairs", "blk", "panel"))),
        check_vma=False,
    )
```
